32 devices in a mesh: gz: 8 (over z, y), gy: 4 (over x, core).
Axes of the slice: x: 2, y: 2, z: 4, core: 2. Of those that a mesh axis runs over, the one named last changes fastest.
Arguments:
- features: bfloat16 [8, 4, 2, 512, 128], P('gz', 'gy'), may hold values from -6 to 6
- brick_sites: int32 [8, 4, 2], P('gz', 'gy'), may hold values from 0 to 8, as said below
- kernel: bfloat16 [27, 128, 128], replicated, may hold values from -0.109375 to 0.109375
- cotangent: bfloat16 [8, 4, 2, 512, 128], P('gz', 'gy'), may hold values from -6 to 6
Outputs:
- act: bfloat16 [8, 4, 2, 512, 128], P('gz', 'gy')
- grad_in: bfloat16 [8, 4, 2, 512, 128], P('gz', 'gy')
- grad_kernel: float32 [27, 128, 128], replicated
The draws below stay inside these ranges and needn't reach their ends.
Inputs may be any that keep to these rules, and one draw needn't show every extreme that they name: `brick_sites`: within a block the places of used slots are distinct; empty slots, marked 8, come after the used ones; every block uses at least 1 slots and some block uses all 2.
All inputs are finite; a program needn't handle non-finite values.
Results may differ from the reference program's by a relative error of at most 0.0049.
Values may be sent and summed in bfloat16 or wider, within the bound.
No kernel may reach another device: no remote copies, remote signals or barrier semaphores. Data moves between devices by JAX's collectives and lax.ppermute only.
A program may use at most 128 MiB of HBM per device.

```python
import jax
import jax.numpy as jnp
from jax import lax

C = 128
TAPS = 27
VOX = 512
BY = 2
BX = 4
NB = 2
SITES = 8
NSZ = 8
NSY = 4


def draw_brick_sites(key, part):
    key_perm, key_count, key_full = jax.random.split(key, 3)
    blocks = NSZ * NSY
    keys = jax.random.split(key_perm, blocks)
    places = jax.vmap(lambda k: jax.random.permutation(k, SITES)[:NB])(keys)
    counts = NB - jax.random.randint(key_count, (blocks,), 0, NB // 2 + 1)
    full_block = jax.random.randint(key_full, (), 0, blocks)
    counts = jnp.where(jnp.arange(blocks) == full_block, NB, counts)
    slots = jnp.arange(NB)[None, :]
    sites = jnp.where(slots < counts[:, None], places, SITES)
    return sites.reshape(NSZ, NSY, NB).astype(jnp.int32)


def block_scale(stream_key, dims, cuts, least, largest):
    level, own = 1.0, jax.random.fold_in(stream_key, 6)
    for dim, blocks in cuts:
        heights = jnp.exp(jax.random.uniform(jax.random.fold_in(own, dim), (blocks,), jnp.float32, least / len(cuts), largest / len(cuts)))
        level = level * jnp.repeat(heights, dims[dim] // blocks).reshape([-1 if axis == dim else 1 for axis in range(len(dims))])
    return level


def gaussian(key, shape, deviation, limit, pieces=(), held_as=jnp.bfloat16):
    result = jax.random.normal(key, shape, jnp.float32) * deviation
    if len(pieces) > 0:
        result = block_scale(key, shape, pieces, -0.22, 0.18) * result
    return jnp.clip(result, min=-limit, max=limit).astype(held_as)


def setup_inputs(seed: int = 0) -> dict:
    key_list = jax.random.split(jax.random.key(seed), 5)
    return {
        "features": gaussian(key_list[0], (NSZ, NSY, NB, VOX, C), 1.0, 6.0, ((0, 8), (1, 4))),
        "brick_sites": draw_brick_sites(jax.random.fold_in(key_list[4], 71), 0),
        "kernel": gaussian(key_list[2], (TAPS, C, C), (TAPS * C) ** -0.5, 0.109375),
        "cotangent": gaussian(key_list[3], (NSZ, NSY, NB, VOX, C), 1.0, 6.0, ((0, 8), (1, 4))),
    }


def tap_offsets():
    return [(dz, dy, dx) for dz in (-1, 0, 1) for dy in (-1, 0, 1) for dx in (-1, 0, 1)]

def build_slab(padded_bricks, padded_sites, index):
    three = lax.dynamic_slice_in_dim(padded_bricks, index, 3, 0)
    three_sites = lax.dynamic_slice_in_dim(padded_sites, index, 3, 0)
    dense = jnp.zeros((3, NSY, SITES + 1, VOX, C), padded_bricks.dtype)
    first = jnp.arange(3, dtype=jnp.int32)[:, None, None]
    second = jnp.arange(NSY, dtype=jnp.int32)[None, :, None]
    dense = dense.at[first, second, three_sites].set(three)[:, :, :SITES]
    dense = dense.reshape(3, NSY, BY, BX, 8, 8, 8, C)
    dense = dense.transpose(0, 4, 1, 2, 5, 3, 6, 7).reshape(24, NSY * BY * 8, BX * 8, C)
    dense = jnp.pad(dense, ((0, 0), (1, 1), (1, 1), (0, 0)))
    return dense[7:17]

def reference(features, brick_sites, kernel, cotangent):
    valid = brick_sites < SITES
    clamped = jnp.minimum(brick_sites, SITES - 1)
    rows_start = ((jnp.arange(NSY, dtype=jnp.int32)[None, :, None] * BY + clamped // BX) * 8).astype(jnp.int32)
    cols_start = (clamped % BX * 8).astype(jnp.int32)
    kernel_full = kernel.astype(jnp.float32)
    offsets = tap_offsets()
    pad_sites = jnp.pad(brick_sites, ((1, 1), (0, 0), (0, 0)), constant_values=SITES)

    def patches_of(slab, index):
        rows = rows_start[index].reshape(-1)
        cols = cols_start[index].reshape(-1)
        zero = jnp.zeros((), jnp.int32)
        return jax.vmap(lambda r, c: lax.dynamic_slice(slab, (zero, r, c, zero), (10, 10, 10, C)))(rows, cols).astype(jnp.float32)
    pad_features = jnp.pad(features, ((1, 1), (0, 0), (0, 0), (0, 0), (0, 0)))

    def forward_row(index):
        slab = build_slab(pad_features, pad_sites, index)
        patches = patches_of(slab, index)
        pre = jnp.zeros((NSY * NB, 8, 8, 8, C), jnp.float32)
        for t, (dz, dy, dx) in enumerate(offsets):
            view = patches[:, 1 + dz:9 + dz, 1 + dy:9 + dy, 1 + dx:9 + dx]
            pre = pre + jnp.einsum('nzyxc,cd->nzyxd', view, kernel_full[t])
        pre = pre.reshape(NSY * NB, VOX, C)
        used = valid[index].reshape(-1)[:, None, None]
        sig = jax.nn.sigmoid(pre)
        act = jnp.where(used, pre * sig, 0.0).astype(jnp.bfloat16)
        upstream = cotangent[index].reshape(NSY * NB, VOX, C).astype(jnp.float32)
        dpre = jnp.where(used, upstream * sig * (1.0 + pre * (1.0 - sig)), 0.0).astype(jnp.bfloat16)
        dpre_cube = dpre.astype(jnp.float32).reshape(NSY * NB, 8, 8, 8, C)
        terms = []
        for t, (dz, dy, dx) in enumerate(offsets):
            view = patches[:, 1 + dz:9 + dz, 1 + dy:9 + dy, 1 + dx:9 + dx]
            terms.append(jnp.einsum('nzyxc,nzyxd->cd', view, dpre_cube))
        return (act, dpre, jnp.stack(terms))
    acts, dpres, kernel_terms = lax.map(forward_row, jnp.arange(NSZ, dtype=jnp.int32))
    dpre_all = dpres.reshape(NSZ, NSY, NB, VOX, C)
    pad_dpre = jnp.pad(dpre_all, ((1, 1), (0, 0), (0, 0), (0, 0), (0, 0)))

    def backward_row(index):
        slab = build_slab(pad_dpre, pad_sites, index)
        patches = patches_of(slab, index)
        grad = jnp.zeros((NSY * NB, 8, 8, 8, C), jnp.float32)
        for t, (dz, dy, dx) in enumerate(offsets):
            view = patches[:, 1 - dz:9 - dz, 1 - dy:9 - dy, 1 - dx:9 - dx]
            grad = grad + jnp.einsum('nzyxd,cd->nzyxc', view, kernel_full[t])
        used = valid[index].reshape(-1)[:, None, None]
        return jnp.where(used, grad.reshape(NSY * NB, VOX, C), 0.0).astype(jnp.bfloat16)
    grads = lax.map(backward_row, jnp.arange(NSZ, dtype=jnp.int32))
    count = jnp.float32(NB * VOX * NSZ * NSY)
    grad_kernel = lax.optimization_barrier(jnp.sum(kernel_terms, axis=0)) / jnp.sqrt(count)
    act = acts.reshape(NSZ, NSY, NB, VOX, C)
    grad_in = grads.reshape(NSZ, NSY, NB, VOX, C)
    return (act, grad_in, grad_kernel)
```

```python
import jax
import jax.numpy as jnp
from jax import lax
from jax.sharding import PartitionSpec as P

C = 128
VOX = 512
BY = 2
BX = 4
NB = 2
SITES = 8


def padded(block, sides, width):
    for axis, dim in sides:
        count = lax.axis_size(axis)
        forward = [(i, i + 1) for i in range(count - 1)]
        backward = [(target, source) for source, target in forward]
        low = lax.ppermute(
            lax.slice_in_dim(block, block.shape[dim] - width, None, axis=dim), axis, forward
        )
        high = lax.ppermute(lax.slice_in_dim(block, 0, width, axis=dim), axis, backward)
        block = jnp.concatenate([low, block, high], axis=dim)
    return block


AXES = ("gz", "gy")


def exchange_plan():
    gz_bits = [("gz", b) for b in range(lax.axis_size("gz").bit_length() - 1)]
    gy_bits = [("gy", b) for b in range(lax.axis_size("gy").bit_length() - 1)]
    groups, gy_bits = [(gy_bits[0],)], gy_bits[1:]
    while gy_bits and gz_bits:
        groups.append((gy_bits.pop(0), gz_bits.pop(0)))
    rest = gy_bits + gz_bits
    while rest:
        groups.append(tuple(rest[:2]))
        rest = rest[2:]
    return groups


def swap_with(value, group, pattern):
    nz, ny = lax.axis_size("gz"), lax.axis_size("gy")
    flip = {"gz": 0, "gy": 0}
    for k, (axis, bit) in enumerate(group):
        if pattern >> k & 1:
            flip[axis] |= 1 << bit
    pairs = [
        (z * ny + y, (z ^ flip["gz"]) * ny + (y ^ flip["gy"]))
        for z in range(nz)
        for y in range(ny)
    ]
    return lax.ppermute(value, AXES, pairs)


def place_in(group):
    place = jnp.zeros((), jnp.int32)
    for k, (axis, bit) in enumerate(group):
        place = place | (((lax.axis_index(axis) >> bit) & 1) << k)
    return place


def scatter_sum(total, plan):
    for level, group in enumerate(plan):
        kind = jnp.float32 if level == 0 else jnp.bfloat16
        count = 1 << len(group)
        me = place_in(group)
        parts = total.reshape(count, -1, C)
        arrived = [
            swap_with(lax.dynamic_index_in_dim(parts, me ^ p, 0, False).astype(kind), group, p)
            for p in range(1, count)
        ]
        total = lax.dynamic_index_in_dim(parts, me, 0, False)
        for piece in arrived:
            total = total + piece.astype(jnp.float32)
    return total


def gather_parts(piece, plan):
    for group in reversed(plan):
        pieces = [piece] + [swap_with(piece, group, p) for p in range(1, 1 << len(group))]
        piece = jnp.concatenate(pieces)
    bits = [b for group in plan for b in reversed(group)]
    piece = piece.reshape((2,) * len(bits) + (-1, C))
    for dim, (axis, bit) in enumerate(bits):
        odd = (lax.axis_index(axis) >> bit) & 1
        piece = jnp.where(odd == 1, jnp.flip(piece, dim), piece)
    return piece.reshape(-1, C)


def sum_over_all(value, scale):
    plan = exchange_plan()
    devices = lax.axis_size("gz") * lax.axis_size("gy")
    rows = value.shape[0] * C
    padded_rows = -(-rows // (16 * devices)) * 16 * devices
    flat = jnp.pad(value.reshape(rows, C), ((0, padded_rows - rows), (0, 0)))
    mine = (scatter_sum(flat, plan) * scale).astype(jnp.bfloat16)
    return gather_parts(mine, plan)[:rows].reshape(value.shape).astype(jnp.float32)


def tap_offsets():
    return [(dz, dy, dx) for dz in (-1, 0, 1) for dy in (-1, 0, 1) for dx in (-1, 0, 1)]


def to_grid(bricks, sites):
    dense = jnp.zeros((SITES + 1, VOX, C), bricks.dtype).at[sites].set(bricks)[:SITES]
    dense = dense.reshape(BY, BX, 8, 8, 8, C).transpose(2, 0, 3, 1, 4, 5)
    return dense.reshape(8, BY * 8, BX * 8, C)


def cut_cubes(volume, rows_start, cols_start, width):
    zero = jnp.zeros((), jnp.int32)
    return jax.vmap(
        lambda r, c: lax.dynamic_slice(volume, (zero, r, c, zero), (width, width, width, C))
    )(rows_start, cols_start)


def local(features, brick_sites, kernel, cotangent):
    bricks = features[0, 0]
    sites = brick_sites[0, 0]
    upstream = cotangent[0, 0]
    valid = (sites < SITES)[:, None, None]
    clamped = jnp.minimum(sites, SITES - 1)
    rows_start = clamped // BX * 8
    cols_start = clamped % BX * 8
    offsets = tap_offsets()
    framed = padded(to_grid(bricks, sites), (("gz", 0), ("gy", 1)), 1)
    framed = jnp.pad(framed, ((0, 0), (0, 0), (1, 1), (0, 0)))
    patches = cut_cubes(framed, rows_start, cols_start, 10)
    pre = jnp.zeros((NB, 8, 8, 8, C), jnp.float32)
    for t, (dz, dy, dx) in enumerate(offsets):
        view = patches[:, 1 + dz : 9 + dz, 1 + dy : 9 + dy, 1 + dx : 9 + dx]
        pre = pre + jnp.einsum(
            "nzyxc,cd->nzyxd", view, kernel[t], preferred_element_type=jnp.float32
        )
    pre = pre.reshape(NB, VOX, C)
    sig = jax.nn.sigmoid(pre)
    act = jnp.where(valid, pre * sig, 0.0).astype(jnp.bfloat16)
    dpre = jnp.where(
        valid, upstream.astype(jnp.float32) * sig * (1.0 + pre * (1.0 - sig)), 0.0
    ).astype(jnp.bfloat16)
    dpre_cube = dpre.reshape(NB, 8, 8, 8, C)
    terms = []
    for t, (dz, dy, dx) in enumerate(offsets):
        view = patches[:, 1 + dz : 9 + dz, 1 + dy : 9 + dy, 1 + dx : 9 + dx]
        terms.append(
            jnp.einsum("nzyxc,nzyxd->cd", view, dpre_cube, preferred_element_type=jnp.float32)
        )
    local_kernel = jnp.stack(terms)
    widened = jnp.pad(dpre_cube, ((0, 0), (2, 2), (2, 2), (2, 2), (0, 0)))
    spread = jnp.zeros((NB, 10, 10, 10, C), jnp.float32)
    for t, (dz, dy, dx) in enumerate(offsets):
        view = widened[:, 1 - dz : 11 - dz, 1 - dy : 11 - dy, 1 - dx : 11 - dx]
        spread = spread + jnp.einsum(
            "nzyxd,cd->nzyxc", view, kernel[t], preferred_element_type=jnp.float32
        )
    canvas = jnp.zeros((10, BY * 8 + 2, BX * 8 + 2, C), jnp.float32)
    zero = jnp.zeros((), jnp.int32)
    for slot in range(NB):
        start = (zero, rows_start[slot], cols_start[slot], zero)
        piece = lax.dynamic_slice(canvas, start, (10, 10, 10, C))
        canvas = lax.dynamic_update_slice(canvas, piece + spread[slot], start)
    canvas = canvas[:, :, 1:-1]
    rims = jnp.concatenate([canvas[0:1], canvas[9:10]], axis=0)
    arrived_rims = padded(rims.astype(jnp.bfloat16), (("gz", 0),), 1).astype(rims.dtype)
    inner = canvas[1:9]
    inner = inner.at[0].add(arrived_rims[0]).at[7].add(arrived_rims[3])
    sides = jnp.concatenate([inner[:, 0:1], inner[:, -1:]], axis=1)
    beside = padded(sides.astype(jnp.bfloat16), (("gy", 1),), 1).astype(sides.dtype)
    core = inner[:, 1:-1]
    core = core.at[:, 0].add(beside[:, 0]).at[:, -1].add(beside[:, 3])
    grad = cut_cubes(core, rows_start, cols_start, 8)
    grad_in = jnp.where(valid, grad.reshape(NB, VOX, C), 0.0).astype(jnp.bfloat16)
    count = NB * VOX * lax.axis_size("gz") * lax.axis_size("gy")
    grad_kernel = sum_over_all(local_kernel, 1.0 / count**0.5)
    return (act[None, None], grad_in[None, None], grad_kernel)


def solution(mesh):
    placed = (
        P("gz", "gy", None, None, None),
        P("gz", "gy", None),
        P(),
        P("gz", "gy", None, None, None),
    )
    return jax.shard_map(
        local,
        mesh=mesh,
        in_specs=placed,
        out_specs=(P("gz", "gy", None, None, None), P("gz", "gy", None, None, None), P()),
        check_vma=False,
    )
```

```python
import functools

import jax
import jax.numpy as jnp
from jax import lax
from jax.experimental import pallas as pl
from jax.experimental.pallas import tpu as pltpu
from jax.sharding import PartitionSpec as P

C = 128
VOX = 512
BY = 2
BX = 4
NB = 2
SITES = 8
TAPS = 27
HALF = 14

AXES = ("gz", "gy")
F32 = jnp.float32
BF16 = jnp.bfloat16

VZ, VY, VX = 12, 20, 48


def exchange_plan():
    gz_bits = [("gz", b) for b in range(lax.axis_size("gz").bit_length() - 1)]
    gy_bits = [("gy", b) for b in range(lax.axis_size("gy").bit_length() - 1)]
    groups, gy_bits = [(gy_bits[0],)], gy_bits[1:]
    while gy_bits and gz_bits:
        groups.append((gy_bits.pop(0), gz_bits.pop(0)))
    rest = gy_bits + gz_bits
    while rest:
        groups.append(tuple(rest[:2]))
        rest = rest[2:]
    return groups


def swap_with(value, group, pattern):
    nz, ny = lax.axis_size("gz"), lax.axis_size("gy")
    flip = {"gz": 0, "gy": 0}
    for k, (axis, bit) in enumerate(group):
        if pattern >> k & 1:
            flip[axis] |= 1 << bit
    pairs = [
        (z * ny + y, (z ^ flip["gz"]) * ny + (y ^ flip["gy"]))
        for z in range(nz)
        for y in range(ny)
    ]
    return lax.ppermute(value, AXES, pairs)


def place_in(group):
    place = jnp.zeros((), jnp.int32)
    for k, (axis, bit) in enumerate(group):
        place = place | (((lax.axis_index(axis) >> bit) & 1) << k)
    return place


def scatter_sum(total, plan):
    for group in plan:
        count = 1 << len(group)
        me = place_in(group)
        parts = total.reshape(count, -1, C)
        arrived = [
            swap_with(lax.dynamic_index_in_dim(parts, me ^ p, 0, False).astype(BF16), group, p)
            for p in range(1, count)
        ]
        total = lax.dynamic_index_in_dim(parts, me, 0, False)
        for piece in arrived:
            total = total + piece.astype(F32)
    return total


def gather_parts(piece, plan):
    for group in reversed(plan):
        pieces = [piece] + [swap_with(piece, group, p) for p in range(1, 1 << len(group))]
        piece = jnp.concatenate(pieces)
    bits = [b for group in plan for b in reversed(group)]
    piece = piece.reshape((2,) * len(bits) + (-1, C))
    for dim, (axis, bit) in enumerate(bits):
        odd = (lax.axis_index(axis) >> bit) & 1
        piece = jnp.where(odd == 1, jnp.flip(piece, dim), piece)
    return piece.reshape(-1, C)


def neighbours(up, down, axis):
    count = lax.axis_size(axis)
    forward = [(i, i + 1) for i in range(count - 1)]
    backward = [(b, a) for a, b in forward]
    return lax.ppermute(up, axis, forward), lax.ppermute(down, axis, backward)


Z_ROWS = NB * 24
Y_ROWS = NB * 24 + 2 * NB * 5


def pack_z_kernel(x_ref, g_ref, up_ref, down_ref):
    for s in range(NB):
        base = 24 * s
        up_ref[base : base + 16] = x_ref[s, 48:64]
        up_ref[base + 16 : base + 24] = g_ref[s, 56:64]
        down_ref[base : base + 16] = x_ref[s, 0:16]
        down_ref[base + 16 : base + 24] = g_ref[s, 0:8]


def pack_z(x, g):
    shape = jax.ShapeDtypeStruct((Z_ROWS, 8, C), BF16)
    return pl.pallas_call(pack_z_kernel, out_shape=(shape, shape), name="pack_z")(x, g)


def pack_y_kernel(x_ref, g_ref, low_ref, high_ref, up_ref, down_ref):
    for s in range(NB):
        base = 24 * s
        for z in range(8):
            up_ref[base + 2 * z : base + 2 * z + 2] = x_ref[s, 8 * z + 6 : 8 * z + 8]
            up_ref[base + 16 + z] = g_ref[s, 8 * z + 7]
            down_ref[base + 2 * z : base + 2 * z + 2] = x_ref[s, 8 * z : 8 * z + 2]
            down_ref[base + 16 + z] = g_ref[s, 8 * z]
    for side, ref in enumerate((low_ref, high_ref)):
        for s in range(NB):
            base = NB * 24 + 10 * side + 5 * s
            src = 24 * s
            for z in range(2):
                up_ref[base + 2 * z : base + 2 * z + 2] = ref[src + 8 * z + 6 : src + 8 * z + 8]
                down_ref[base + 2 * z : base + 2 * z + 2] = ref[src + 8 * z : src + 8 * z + 2]
            up_ref[base + 4] = ref[src + 16 + 7]
            down_ref[base + 4] = ref[src + 16]


def pack_y(x, g, low, high):
    shape = jax.ShapeDtypeStruct((Y_ROWS, 8, C), BF16)
    return pl.pallas_call(pack_y_kernel, out_shape=(shape, shape), name="pack_y")(x, g, low, high)


def clear(ref):
    rows = ref.shape[0]
    flat = jnp.zeros((1,) + ref.shape[1:], ref.dtype)
    for z in range(rows):
        ref[z : z + 1] = flat


def place_of(site):
    inside = jnp.minimum(site, SITES - 1)
    return inside // BX, pl.multiple_of(inside % BX * 8 + 8, 8)


def fill(vol, codes, x_ref, zl_ref, zh_ref, yl_ref, yh_ref):
    def put(z0, y0, x0, rows):
        vol[z0 : z0 + rows.shape[0], pl.ds(y0, rows.shape[1]), pl.ds(x0, 8)] = rows.astype(F32)

    for s in range(NB):
        site = codes[0, s]
        py, px = place_of(site)

        @pl.when(site < SITES)
        def _():
            put(2, 2 + 8 * py, px, x_ref[s].reshape(8, 8, 8, C))

        for side, ref in ((1, zl_ref), (2, zh_ref)):
            zsite = codes[side, s]
            zpy, zpx = place_of(zsite)

            @pl.when(zsite < SITES)
            def _(ref=ref, side=side, zpy=zpy, zpx=zpx, s=s):
                put(0 if side == 1 else 10, 2 + 8 * zpy, zpx, ref[24 * s : 24 * s + 16].reshape(2, 8, 8, C))

        for first, ref, row, y0 in ((3, yl_ref, 1, 0), (6, yh_ref, 0, 18)):
            for k, (z0, base, depth) in enumerate(
                ((2, 24 * s, 8), (0, 48 + 5 * s, 2), (10, 58 + 5 * s, 2))
            ):
                ysite = codes[first + k, s]
                ypy, ypx = place_of(ysite)

                @pl.when((ysite < SITES) & (ypy == row))
                def _(ref=ref, z0=z0, y0=y0, base=base, depth=depth, ypx=ypx):
                    put(z0, y0, ypx, ref[base : base + 2 * depth].reshape(depth, 2, 8, C))


def stack_x(vol, dst, dst_at, z0, y0s, x0s, nz, ny):
    for z in range(nz):
        for y in range(ny):
            halves = []
            for y0, x0 in zip(y0s, x0s):
                row = vol[z0 + z, y0 + y, pl.ds(x0 - 8, 24)]
                halves.append(
                    jnp.concatenate([row[7:15], row[8:16], row[9:17]], axis=1)
                )
            dst[dst_at + z * ny + y] = jnp.concatenate(halves, axis=0).astype(BF16)


def views(stack, base, ny_all, nz, ny):
    result = []
    for dz in range(3):
        for dy in range(3):
            planes = [
                stack[base + (z + dz) * ny_all + dy : base + (z + dz) * ny_all + dy + ny]
                for z in range(nz)
            ]
            result.append(jnp.concatenate(planes, axis=0).reshape(nz * ny * 16, 3 * C))
    return result


def dot(a, b, dims=((1,), (0,))):
    return lax.dot_general(a, b, (dims, ((), ())), preferred_element_type=F32)


def convolve(stack, base, ny_all, nz, ny, weight):
    total = None
    for k, view in enumerate(views(stack, base, ny_all, nz, ny)):
        term = weight(k, view)
        total = term if total is None else total + term
    return total


def forward_kernel(codes, core, x_ref, g_ref, zl_ref, zh_ref, yl_ref, yh_ref, w_ref,
                   act_ref, dpre_ref, keep_ref, send_ref, vol, stack, turned):
    clear(vol)
    fill(vol, codes, x_ref, zl_ref, zh_ref, yl_ref, yh_ref)
    places = [place_of(codes[0, s]) for s in range(NB)]
    stack_x(vol, stack, 0, 1, [1 + 8 * py for py, _ in places], [px for _, px in places], 10, 10)

    def weight(k, view):
        return dot(view, w_ref[3 * k : 3 * k + 3].reshape(3 * C, C))

    used = [codes[0, s] < SITES for s in range(NB)]
    for half in range(2):
        pre = convolve(stack, 40 * half, 10, 4, 8, weight)
        sig = 1.0 / (1.0 + jnp.exp(-pre))
        act = (pre * sig).reshape(32, 16, C)
        slope = (sig * (1.0 + pre * (1.0 - sig))).reshape(32, 16, C)
        both = []
        for s in range(NB):
            rows = slice(32 * half, 32 * half + 32)
            a = jnp.where(used[s], act[:, 8 * s : 8 * s + 8], 0.0)
            act_ref[s, rows] = a.astype(BF16)
            d = g_ref[s, rows].astype(F32) * slope[:, 8 * s : 8 * s + 8]
            both.append(jnp.where(used[s], d, 0.0))
        d = jnp.concatenate(both, axis=1).astype(BF16)
        dpre_ref[32 * half : 32 * half + 32] = d
        turned[:, 512 * half : 512 * half + 512] = d.reshape(512, C).T

    dt = turned[...]
    for k in range(9):
        dz, dy = divmod(k, 3)
        planes = [stack[(z + dz) * 10 + dy : (z + dz) * 10 + dy + 8] for z in range(8)]
        view = jnp.concatenate(planes, axis=0).reshape(1024, 3 * C)
        term = dot(dt, view)
        for dx in range(3):
            t = 3 * k + dx
            value = term[:, C * dx : C * dx + C].T
            half, at = divmod(t, HALF)

            @pl.when(core[0] == half)
            def _(value=value, at=at):
                keep_ref[at] = value

            @pl.when(core[0] != half)
            def _(value=value, at=at):
                send_ref[at] = value.astype(BF16)
    for t in range(TAPS, 2 * HALF):
        half, at = divmod(t, HALF)

        @pl.when(core[0] == half)
        def _(at=at):
            keep_ref[at] = jnp.zeros((C, C), F32)

        @pl.when(core[0] != half)
        def _(at=at):
            send_ref[at] = jnp.zeros((C, C), BF16)


SMEM = pl.BlockSpec(memory_space=pltpu.SMEM)
VMEM = pl.BlockSpec(memory_space=pltpu.VMEM)


def forward(codes, core, x, g, zl, zh, yl, yh, w):
    rows = jax.ShapeDtypeStruct((NB, 64, 8, C), BF16)
    return pl.pallas_call(
        forward_kernel,
        out_shape=(
            rows,
            jax.ShapeDtypeStruct((64, 16, C), BF16),
            jax.ShapeDtypeStruct((HALF, C, C), F32),
            jax.ShapeDtypeStruct((HALF, C, C), BF16),
        ),
        in_specs=[SMEM, SMEM] + [VMEM] * 7,
        out_specs=(VMEM,) * 4,
        scratch_shapes=[
            pltpu.VMEM((VZ, VY, VX, C), F32),
            pltpu.VMEM((100, 16, 3 * C), BF16),
            pltpu.VMEM((C, 1024), BF16),
        ],
        compiler_params=pltpu.CompilerParams(vmem_limit_bytes=40 << 20),
        cost_estimate=pl.CostEstimate(flops=2 * 10**9, bytes_accessed=5 << 20, transcendentals=1 << 17),
        name="forward",
    )(codes, core, x, g, zl, zh, yl, yh, w)


def backward_kernel(codes, x_ref, dpre_ref, zl_ref, zh_ref, yl_ref, yh_ref, w_ref,
                    grad_ref, vol, stack):
    clear(vol)
    fill(vol, codes, x_ref, zl_ref, zh_ref, yl_ref, yh_ref)

    def weight(k, view):
        return dot(view, w_ref[3 * k : 3 * k + 3].reshape(3 * C, C))

    jobs = []
    for block, z in ((1, 1), (2, 10)):
        jobs.append((block, z, None, 1, 8))
    for first, y in ((3, 1), (6, 18)):
        jobs.append((first, 2, y, 8, 1))
        jobs.append((first + 1, 1, y, 1, 1))
        jobs.append((first + 2, 10, y, 1, 1))
    base = 0
    found = []
    for block, z0, y0, nz, ny in jobs:
        places = [place_of(codes[block, s]) for s in range(NB)]
        y0s = [2 + 8 * py if y0 is None else y0 for py, _ in places]
        x0s = [px for _, px in places]
        stack_x(vol, stack, base, z0 - 1, [y - 1 for y in y0s], x0s, nz + 2, ny + 2)
        pre = convolve(stack, base, ny + 2, nz, ny, weight)
        sig = 1.0 / (1.0 + jnp.exp(-pre))
        slope = (sig * (1.0 + pre * (1.0 - sig))).reshape(nz, ny, 16, C)
        found.append((block, z0, y0, nz, ny, y0s, x0s, slope))
        base += (nz + 2) * (ny + 2)
    values = []
    for block, z0, y0, nz, ny, y0s, x0s, slope in found:
        for s in range(NB):
            if block == 1:
                g = zl_ref[24 * s + 16 : 24 * s + 24]
            elif block == 2:
                g = zh_ref[24 * s + 16 : 24 * s + 24]
            else:
                ref = yl_ref if block < 6 else yh_ref
                kind = (block - 3) % 3
                if kind == 0:
                    g = ref[24 * s + 16 : 24 * s + 24]
                else:
                    at = 48 + 10 * (kind - 1) + 5 * s + 4
                    g = ref[at : at + 1]
            g = g.astype(F32).reshape(nz, ny, 8, C)
            value = (g * slope[:, :, 8 * s : 8 * s + 8]).astype(BF16).astype(F32)
            values.append(value)

    clear(vol)
    for s in range(NB):
        site = codes[0, s]
        py, px = place_of(site)

        @pl.when(site < SITES)
        def _(s=s, py=py, px=px):
            own = dpre_ref[...].astype(F32).reshape(8, 8, 16, C)[:, :, 8 * s : 8 * s + 8]
            vol[2:10, pl.ds(2 + 8 * py, 8), pl.ds(px, 8)] = own

    at = 0
    for block, z0, y0, nz, ny, y0s, x0s, slope in found:
        for s in range(NB):
            site = codes[block, s]
            py, px = place_of(site)
            ok = site < SITES
            if block >= 3:
                ok = ok & (py == (1 if block < 6 else 0))
            value = values[at]
            at += 1

            @pl.when(ok)
            def _(value=value, z0=z0, nz=nz, ny=ny, y0=y0s[s], x0=x0s[s]):
                vol[z0 : z0 + nz, pl.ds(y0, ny), pl.ds(x0, 8)] = value

    places = [place_of(codes[0, s]) for s in range(NB)]
    stack_x(vol, stack, 0, 1, [1 + 8 * py for py, _ in places], [px for _, px in places], 10, 10)

    def back(k, view):
        turned = [w_ref[26 - 3 * k - dx] for dx in range(3)]
        return dot(view, jnp.concatenate(turned, axis=1), ((1,), (1,)))

    for half in range(2):
        grad = convolve(stack, 40 * half, 10, 4, 8, back).reshape(32, 16, C)
        for s in range(NB):
            value = jnp.where(codes[0, s] < SITES, grad[:, 8 * s : 8 * s + 8], 0.0)
            grad_ref[s, 32 * half : 32 * half + 32] = value.astype(BF16)


def backward(codes, x, dpre, zl, zh, yl, yh, w):
    return pl.pallas_call(
        backward_kernel,
        out_shape=jax.ShapeDtypeStruct((NB, 64, 8, C), BF16),
        in_specs=[SMEM] + [VMEM] * 7,
        out_specs=VMEM,
        scratch_shapes=[
            pltpu.VMEM((VZ, VY, VX, C), F32),
            pltpu.VMEM((160, 16, 3 * C), BF16),
        ],
        compiler_params=pltpu.CompilerParams(vmem_limit_bytes=40 << 20),
        cost_estimate=pl.CostEstimate(flops=10**9, bytes_accessed=5 << 20, transcendentals=1 << 16),
        name="backward",
    )(codes, x, dpre, zl, zh, yl, yh, w)


def local(features, brick_sites, kernel, cotangent):
    x = features.reshape(NB, 64, 8, C)
    g = cotangent.reshape(NB, 64, 8, C)
    sites = brick_sites.reshape(NB)
    devices = lax.axis_size("gz") * lax.axis_size("gy")
    up, down = pack_z(x, g)
    zl, zh = neighbours(up, down, "gz")
    own_code = SITES - sites
    code_l, code_h = neighbours(own_code, own_code, "gz")
    trio = jnp.stack([own_code, code_l, code_h])
    up, down = pack_y(x, g, zl, zh)
    yl, yh = neighbours(up, down, "gy")
    trio_l, trio_h = neighbours(trio, trio, "gy")
    codes = SITES - jnp.concatenate([trio, trio_l, trio_h])
    core = (lax.axis_index("gy") & 1).reshape(1).astype(jnp.int32)
    act, dpre, keep, send = forward(codes, core, x, g, zl, zh, yl, yh, kernel)
    grad_in = backward(codes, x, dpre, zl, zh, yl, yh, kernel)

    plan = exchange_plan()
    rows = TAPS * C
    share = 16 * devices
    padded_rows = -(-(2 * HALF * C) // share) * share
    arrived = swap_with(send, plan[0], 1)
    total = (keep + arrived.astype(F32)).reshape(HALF * C, C)
    total = jnp.pad(total, ((0, padded_rows // 2 - HALF * C), (0, 0)))
    scale = 1.0 / (NB * VOX * devices) ** 0.5
    mine = (scatter_sum(total, plan[1:]) * scale).astype(BF16)
    halves = gather_parts(mine, plan).reshape(2, padded_rows // 2, C)
    grad_kernel = halves[:, : HALF * C].reshape(-1, C)[:rows].reshape(TAPS, C, C).astype(F32)
    shape = (1, 1, NB, VOX, C)
    return act.reshape(shape), grad_in.reshape(shape), grad_kernel


def solution(mesh):
    placed = (
        P("gz", "gy", None, None, None),
        P("gz", "gy", None),
        P(),
        P("gz", "gy", None, None, None),
    )
    return jax.shard_map(
        local,
        mesh=mesh,
        in_specs=placed,
        out_specs=(P("gz", "gy", None, None, None), P("gz", "gy", None, None, None), P()),
        check_vma=False,
    )
```

```python
import functools

import jax
import jax.numpy as jnp
from jax import lax
from jax.experimental import pallas as pl
from jax.experimental.pallas import tpu as pltpu
from jax.sharding import PartitionSpec as P

C = 128
VOX = 512
BY = 2
BX = 4
NB = 2
SITES = 8
TAPS = 27
HALF = 14

AXES = ("gz", "gy")
F32 = jnp.float32
BF16 = jnp.bfloat16

VZ, VY, VX = 12, 20, 48

SMEM = pl.BlockSpec(memory_space=pltpu.SMEM)
VMEM = pl.BlockSpec(memory_space=pltpu.VMEM)
ANY = pl.BlockSpec(memory_space=pl.ANY)


def exchange_plan():
    gz_bits = [("gz", b) for b in range(lax.axis_size("gz").bit_length() - 1)]
    gy_bits = [("gy", b) for b in range(lax.axis_size("gy").bit_length() - 1)]
    groups, gy_bits = [(gy_bits[0],)], gy_bits[1:]
    while gy_bits and gz_bits:
        groups.append((gy_bits.pop(0), gz_bits.pop(0)))
    rest = gy_bits + gz_bits
    while rest:
        groups.append(tuple(rest[:2]))
        rest = rest[2:]
    return groups


def swap_with(value, group, pattern):
    nz, ny = lax.axis_size("gz"), lax.axis_size("gy")
    flip = {"gz": 0, "gy": 0}
    for k, (axis, bit) in enumerate(group):
        if pattern >> k & 1:
            flip[axis] |= 1 << bit
    pairs = [
        (z * ny + y, (z ^ flip["gz"]) * ny + (y ^ flip["gy"]))
        for z in range(nz)
        for y in range(ny)
    ]
    return lax.ppermute(value, AXES, pairs)


def place_in(group):
    place = jnp.zeros((), jnp.int32)
    for k, (axis, bit) in enumerate(group):
        place = place | (((lax.axis_index(axis) >> bit) & 1) << k)
    return place


def part_of(parts, index):
    return lax.dynamic_index_in_dim(parts, index, 0, False)


def exchange_sum(total, group, ahead=None):
    count = 1 << len(group)
    me = place_in(group)
    parts = total.reshape(count, -1, C)
    arrived = [
        swap_with(part_of(parts, me ^ p).astype(BF16), group, p) for p in range(1, count)
    ]
    total = part_of(parts, me)
    if ahead is not None:
        arrived = ahead(arrived)
    for piece in arrived:
        total = total + piece.astype(F32)
    return total


def neighbours(up, down, axis):
    count = lax.axis_size(axis)
    forward = [(i, i + 1) for i in range(count - 1)]
    backward = [(b, a) for a, b in forward]
    return lax.ppermute(up, axis, forward), lax.ppermute(down, axis, backward)


Z_ROWS = NB * 24 + 1
Y_ROWS = NB * 24 + 2 * NB * 5 + 3


def pack_z_kernel(sites_ref, x_ref, g_ref, up_ref, down_ref, beside_up, beside_down, sites, sems):
    moves = [(sites_ref, sites)]
    for s in range(NB):
        base = 24 * s
        first, last = slice(base, base + 16), slice(base + 16, base + 24)
        moves += [
            (x_ref.at[s, 6:8], up_ref.at[first].reshape(2, 8, 8, C)),
            (g_ref.at[s, 7], up_ref.at[last]),
            (x_ref.at[s, 0:2], down_ref.at[first].reshape(2, 8, 8, C)),
            (g_ref.at[s, 0], down_ref.at[last]),
            (x_ref.at[s, :, 6:8], beside_up.at[first].reshape(8, 2, 8, C)),
            (g_ref.at[s, :, 7], beside_up.at[last]),
            (x_ref.at[s, :, 0:2], beside_down.at[first].reshape(8, 2, 8, C)),
            (g_ref.at[s, :, 0], beside_down.at[last]),
        ]
    copies = [
        pltpu.make_async_copy(src, dst, sems.at[k]) for k, (src, dst) in enumerate(moves)
    ]
    for copy in copies:
        copy.start()
    copies[0].wait()
    lane = lax.broadcasted_iota(jnp.int32, (8, C), 1)
    code = jnp.zeros((8, C), jnp.int32)
    for s in range(NB):
        code = jnp.where(lane == s, SITES - sites[s], code)
    code = code.astype(F32).astype(BF16)
    up_ref[Z_ROWS - 1] = code
    down_ref[Z_ROWS - 1] = code
    for copy in copies[1:]:
        copy.wait()


def small(limit):
    return pltpu.CompilerParams(vmem_limit_bytes=limit << 20)


def pack_z(sites, x, g):
    shape = jax.ShapeDtypeStruct((Z_ROWS, 8, C), BF16)
    beside = jax.ShapeDtypeStruct((NB * 24, 8, C), BF16)
    return pl.pallas_call(
        pack_z_kernel,
        out_shape=(shape, shape, beside, beside),
        in_specs=[ANY, ANY, ANY],
        out_specs=(VMEM,) * 4,
        scratch_shapes=[pltpu.SMEM((NB,), jnp.int32), pltpu.SemaphoreType.DMA((1 + 8 * NB,))],
        compiler_params=small(4),
        name="pack_z",
    )(sites, x, g)


def pack_y_kernel(own_up, own_down, mine_ref, low_ref, high_ref, up_ref, down_ref):
    up_ref[: NB * 24] = own_up[...]
    down_ref[: NB * 24] = own_down[...]
    for side, ref in enumerate((low_ref, high_ref)):
        for s in range(NB):
            base = NB * 24 + 10 * side + 5 * s
            src = 24 * s
            for z in range(2):
                up_ref[base + 2 * z : base + 2 * z + 2] = ref[src + 8 * z + 6 : src + 8 * z + 8]
                down_ref[base + 2 * z : base + 2 * z + 2] = ref[src + 8 * z : src + 8 * z + 2]
            up_ref[base + 4] = ref[src + 16 + 7]
            down_ref[base + 4] = ref[src + 16]
    for k, ref in enumerate((mine_ref, low_ref, high_ref)):
        up_ref[Y_ROWS - 3 + k] = ref[Z_ROWS - 1]
        down_ref[Y_ROWS - 3 + k] = ref[Z_ROWS - 1]


def pack_y(own_up, own_down, mine, low, high):
    shape = jax.ShapeDtypeStruct((Y_ROWS, 8, C), BF16)
    return pl.pallas_call(
        pack_y_kernel,
        out_shape=(shape, shape),
        in_specs=[VMEM] * 5,
        out_specs=(VMEM, VMEM),
        compiler_params=small(4),
        name="pack_y",
    )(own_up, own_down, mine, low, high)


def clear(ref):
    rows = ref.shape[0]
    flat = jnp.zeros((1,) + ref.shape[1:], ref.dtype)
    for z in range(rows):
        ref[z : z + 1] = flat


def place_of(site):
    inside = jnp.minimum(site, SITES - 1)
    return inside // BX, pl.multiple_of(inside % BX * 8 + 8, 8)


def fill(vol, codes, x_ref, zl_ref, zh_ref, yl_ref, yh_ref):
    def put(z0, y0, x0, rows):
        vol[z0 : z0 + rows.shape[0], pl.ds(y0, rows.shape[1]), pl.ds(x0, 8)] = rows.astype(F32)

    for s in range(NB):
        site = codes[0, s]
        py, px = place_of(site)

        @pl.when(site < SITES)
        def _():
            put(2, 2 + 8 * py, px, x_ref[s])

        for side, ref in ((1, zl_ref), (2, zh_ref)):
            zsite = codes[side, s]
            zpy, zpx = place_of(zsite)

            @pl.when(zsite < SITES)
            def _(ref=ref, side=side, zpy=zpy, zpx=zpx, s=s):
                put(0 if side == 1 else 10, 2 + 8 * zpy, zpx, ref[24 * s : 24 * s + 16].reshape(2, 8, 8, C))

        for first, ref, row, y0 in ((3, yl_ref, 1, 0), (6, yh_ref, 0, 18)):
            for k, (z0, base, depth) in enumerate(
                ((2, 24 * s, 8), (0, 48 + 5 * s, 2), (10, 58 + 5 * s, 2))
            ):
                ysite = codes[first + k, s]
                ypy, ypx = place_of(ysite)

                @pl.when((ysite < SITES) & (ypy == row))
                def _(ref=ref, z0=z0, y0=y0, base=base, depth=depth, ypx=ypx):
                    put(z0, y0, ypx, ref[base : base + 2 * depth].reshape(depth, 2, 8, C))


def stack_x(vol, dst, dst_at, z0, y0s, x0s, nz, ny):
    for z in range(nz):
        for y in range(ny):
            halves = []
            for y0, x0 in zip(y0s, x0s):
                row = vol[z0 + z, y0 + y, pl.ds(x0 - 8, 24)]
                halves.append(
                    jnp.concatenate([row[7:15], row[8:16], row[9:17]], axis=1)
                )
            dst[dst_at + z * ny + y] = jnp.concatenate(halves, axis=0).astype(BF16)


def views(stack, base, ny_all, nz, ny):
    result = []
    for dz in range(3):
        for dy in range(3):
            planes = [
                stack[base + (z + dz) * ny_all + dy : base + (z + dz) * ny_all + dy + ny]
                for z in range(nz)
            ]
            result.append(jnp.concatenate(planes, axis=0).reshape(nz * ny * 16, 3 * C))
    return result


def dot(a, b, dims=((1,), (0,))):
    return lax.dot_general(a, b, (dims, ((), ())), preferred_element_type=F32)


def convolve(stack, base, ny_all, nz, ny, weight):
    total = None
    for k, view in enumerate(views(stack, base, ny_all, nz, ny)):
        term = weight(k, view)
        total = term if total is None else total + term
    return total


def forward_kernel(codes, core, x_hbm, g_hbm, zl_ref, zh_ref, yl_ref, yh_ref, w_hbm,
                   act_ref, dpre_ref, keep_ref, send_ref, vol, stack, turned, x_ref, g_ref, w_ref, sems):
    copies = [
        pltpu.make_async_copy(src, dst, sems.at[k])
        for k, (src, dst) in enumerate(((x_hbm, x_ref), (w_hbm, w_ref), (g_hbm, g_ref)))
    ]
    for copy in copies:
        copy.start()
    clear(vol)
    copies[0].wait()
    fill(vol, codes, x_ref, zl_ref, zh_ref, yl_ref, yh_ref)
    places = [place_of(codes[0, s]) for s in range(NB)]
    stack_x(vol, stack, 0, 1, [1 + 8 * py for py, _ in places], [px for _, px in places], 10, 10)

    def weight(k, view):
        return dot(view, w_ref[3 * k : 3 * k + 3].reshape(3 * C, C))

    used = [codes[0, s] < SITES for s in range(NB)]
    copies[1].wait()
    copies[2].wait()
    for half in range(2):
        pre = convolve(stack, 40 * half, 10, 4, 8, weight)
        sig = 1.0 / (1.0 + jnp.exp(-pre))
        act = (pre * sig).reshape(32, 16, C)
        slope = (sig * (1.0 + pre * (1.0 - sig))).reshape(32, 16, C)
        both = []
        for s in range(NB):
            rows = slice(32 * half, 32 * half + 32)
            a = jnp.where(used[s], act[:, 8 * s : 8 * s + 8], 0.0)
            act_ref[s, rows] = a.astype(BF16)
            d = g_ref[s, 4 * half : 4 * half + 4].astype(F32).reshape(32, 8, C) * slope[:, 8 * s : 8 * s + 8]
            both.append(jnp.where(used[s], d, 0.0))
        d = jnp.concatenate(both, axis=1).astype(BF16)
        dpre_ref[32 * half : 32 * half + 32] = d
        turned[:, 512 * half : 512 * half + 512] = d.reshape(512, C).T

    dt = turned[...]
    for k in range(9):
        dz, dy = divmod(k, 3)
        planes = [stack[(z + dz) * 10 + dy : (z + dz) * 10 + dy + 8] for z in range(8)]
        view = jnp.concatenate(planes, axis=0).reshape(1024, 3 * C)
        term = dot(dt, view)
        for dx in range(3):
            t = 3 * k + dx
            value = term[:, C * dx : C * dx + C].T
            half, at = divmod(t, HALF)

            @pl.when(core[0] == half)
            def _(value=value, at=at):
                keep_ref[at] = value

            @pl.when(core[0] != half)
            def _(value=value, at=at):
                send_ref[at] = value.astype(BF16)
    for t in range(TAPS, 2 * HALF):
        half, at = divmod(t, HALF)

        @pl.when(core[0] == half)
        def _(at=at):
            keep_ref[at] = jnp.zeros((C, C), F32)

        @pl.when(core[0] != half)
        def _(at=at):
            send_ref[at] = jnp.zeros((C, C), BF16)


def forward(codes, core, x, g, zl, zh, yl, yh, w):
    rows = jax.ShapeDtypeStruct((NB, 64, 8, C), BF16)
    return pl.pallas_call(
        forward_kernel,
        out_shape=(
            rows,
            jax.ShapeDtypeStruct((64, 16, C), BF16),
            jax.ShapeDtypeStruct((HALF, C, C), F32),
            jax.ShapeDtypeStruct((HALF, C, C), BF16),
        ),
        in_specs=[SMEM, SMEM, ANY, ANY] + [VMEM] * 4 + [ANY],
        out_specs=(VMEM,) * 4,
        scratch_shapes=[
            pltpu.VMEM((VZ, VY, VX, C), F32),
            pltpu.VMEM((100, 16, 3 * C), BF16),
            pltpu.VMEM((C, 1024), BF16),
            pltpu.VMEM((NB, 8, 8, 8, C), BF16),
            pltpu.VMEM((NB, 8, 8, 8, C), BF16),
            pltpu.VMEM((TAPS, C, C), BF16),
            pltpu.SemaphoreType.DMA((3,)),
        ],
        compiler_params=small(24),
        cost_estimate=pl.CostEstimate(flops=2 * 10**9, bytes_accessed=5 << 20, transcendentals=1 << 17),
        name="forward",
    )(codes, core, x, g, zl, zh, yl, yh, w)


def backward_kernel(codes, x_hbm, dpre_ref, zl_ref, zh_ref, yl_ref, yh_ref, w_hbm,
                    grad_ref, vol, stack, x_ref, w_ref, sems):
    copies = [
        pltpu.make_async_copy(src, dst, sems.at[k])
        for k, (src, dst) in enumerate(((x_hbm, x_ref), (w_hbm, w_ref)))
    ]
    for copy in copies:
        copy.start()
    clear(vol)
    for copy in copies:
        copy.wait()
    fill(vol, codes, x_ref, zl_ref, zh_ref, yl_ref, yh_ref)

    def weight(k, view):
        return dot(view, w_ref[3 * k : 3 * k + 3].reshape(3 * C, C))

    jobs = []
    for block, z in ((1, 1), (2, 10)):
        jobs.append((block, z, None, 1, 8))
    for first, y in ((3, 1), (6, 18)):
        jobs.append((first, 2, y, 8, 1))
        jobs.append((first + 1, 1, y, 1, 1))
        jobs.append((first + 2, 10, y, 1, 1))
    base = 0
    found = []
    for block, z0, y0, nz, ny in jobs:
        places = [place_of(codes[block, s]) for s in range(NB)]
        y0s = [2 + 8 * py if y0 is None else y0 for py, _ in places]
        x0s = [px for _, px in places]
        stack_x(vol, stack, base, z0 - 1, [y - 1 for y in y0s], x0s, nz + 2, ny + 2)
        pre = convolve(stack, base, ny + 2, nz, ny, weight)
        sig = 1.0 / (1.0 + jnp.exp(-pre))
        slope = (sig * (1.0 + pre * (1.0 - sig))).reshape(nz, ny, 16, C)
        found.append((block, z0, y0, nz, ny, y0s, x0s, slope))
        base += (nz + 2) * (ny + 2)
    values = []
    for block, z0, y0, nz, ny, y0s, x0s, slope in found:
        for s in range(NB):
            if block == 1:
                g = zl_ref[24 * s + 16 : 24 * s + 24]
            elif block == 2:
                g = zh_ref[24 * s + 16 : 24 * s + 24]
            else:
                ref = yl_ref if block < 6 else yh_ref
                kind = (block - 3) % 3
                if kind == 0:
                    g = ref[24 * s + 16 : 24 * s + 24]
                else:
                    at = 48 + 10 * (kind - 1) + 5 * s + 4
                    g = ref[at : at + 1]
            g = g.astype(F32).reshape(nz, ny, 8, C)
            value = (g * slope[:, :, 8 * s : 8 * s + 8]).astype(BF16).astype(F32)
            values.append(value)

    clear(vol)
    for s in range(NB):
        site = codes[0, s]
        py, px = place_of(site)

        @pl.when(site < SITES)
        def _(s=s, py=py, px=px):
            own = dpre_ref[...].astype(F32).reshape(8, 8, 16, C)[:, :, 8 * s : 8 * s + 8]
            vol[2:10, pl.ds(2 + 8 * py, 8), pl.ds(px, 8)] = own

    at = 0
    for block, z0, y0, nz, ny, y0s, x0s, slope in found:
        for s in range(NB):
            site = codes[block, s]
            py, px = place_of(site)
            ok = site < SITES
            if block >= 3:
                ok = ok & (py == (1 if block < 6 else 0))
            value = values[at]
            at += 1

            @pl.when(ok)
            def _(value=value, z0=z0, nz=nz, ny=ny, y0=y0s[s], x0=x0s[s]):
                vol[z0 : z0 + nz, pl.ds(y0, ny), pl.ds(x0, 8)] = value

    places = [place_of(codes[0, s]) for s in range(NB)]
    stack_x(vol, stack, 0, 1, [1 + 8 * py for py, _ in places], [px for _, px in places], 10, 10)

    def back(k, view):
        turned = [w_ref[26 - 3 * k - dx] for dx in range(3)]
        return dot(view, jnp.concatenate(turned, axis=1), ((1,), (1,)))

    for half in range(2):
        grad = convolve(stack, 40 * half, 10, 4, 8, back).reshape(32, 16, C)
        for s in range(NB):
            value = jnp.where(codes[0, s] < SITES, grad[:, 8 * s : 8 * s + 8], 0.0)
            grad_ref[s, 32 * half : 32 * half + 32] = value.astype(BF16)


def backward(codes, x, dpre, zl, zh, yl, yh, w):
    return pl.pallas_call(
        backward_kernel,
        out_shape=jax.ShapeDtypeStruct((NB, 64, 8, C), BF16),
        in_specs=[SMEM, ANY] + [VMEM] * 5 + [ANY],
        out_specs=VMEM,
        scratch_shapes=[
            pltpu.VMEM((VZ, VY, VX, C), F32),
            pltpu.VMEM((160, 16, 3 * C), BF16),
            pltpu.VMEM((NB, 8, 8, 8, C), BF16),
            pltpu.VMEM((TAPS, C, C), BF16),
            pltpu.SemaphoreType.DMA((2,)),
        ],
        compiler_params=small(24),
        cost_estimate=pl.CostEstimate(flops=10**9, bytes_accessed=5 << 20, transcendentals=1 << 16),
        name="backward",
    )(codes, x, dpre, zl, zh, yl, yh, w)


def finish_kernel(first, share, sizes, me, *refs):
    pieces, out = refs[:-1], refs[-1]
    middle, inner_sizes = sizes[1], sizes[2:]
    inner = 1
    for n in inner_sizes:
        inner *= n
    for k, ref in enumerate(pieces):
        half = (k // middle) ^ me[0]
        outer = (k % middle) ^ me[1]
        for r in range(inner):
            block, stride, rest = outer * inner, inner, r
            for level, n in enumerate(inner_sizes):
                stride //= n
                digit, rest = divmod(rest, stride)
                block = block + (digit ^ me[2 + level]) * stride
            value = ref[r * share : (r + 1) * share].astype(F32)
            for h in range(2):
                whole, rem = divmod(min(first, TAPS * C - h * first), share)

                @pl.when((half == h) & (block < whole))
                def _(value=value, h=h, block=block):
                    out[pl.ds(pl.multiple_of(h * first + block * share, 8), share)] = value

                if rem:

                    @pl.when((half == h) & (block == whole))
                    def _(value=value, h=h, whole=whole, rem=rem):
                        at = h * first + whole * share
                        out[at : at + rem] = value[:rem]


def finish(first, share, plan, pieces):
    sizes = [1 << len(group) for group in plan]
    me = jnp.stack([place_in(group) for group in plan])
    return pl.pallas_call(
        functools.partial(finish_kernel, first, share, sizes),
        out_shape=jax.ShapeDtypeStruct((TAPS * C, C), F32),
        in_specs=[SMEM] + [VMEM] * len(pieces),
        out_specs=VMEM,
        compiler_params=small(8),
        name="finish",
    )(me, *pieces)


def local(features, brick_sites, kernel, cotangent):
    x = features.reshape(NB, 8, 8, 8, C)
    g = cotangent.reshape(NB, 8, 8, 8, C)
    sites = brick_sites.reshape(NB)
    devices = lax.axis_size("gz") * lax.axis_size("gy")
    z_up, z_down, own_up, own_down = pack_z(sites, x, g)
    zl, zh = neighbours(z_up, z_down, "gz")
    y_up, y_down = pack_y(own_up, own_down, z_up, zl, zh)
    yl, yh = neighbours(y_up, y_down, "gy")
    codes = jnp.concatenate(
        [sites[None]]
        + [SITES - m[rows:, 0, :NB].astype(jnp.int32)
           for m, rows in ((zl, Z_ROWS - 1), (zh, Z_ROWS - 1), (yl, Y_ROWS - 3), (yh, Y_ROWS - 3))]
    )
    core = (lax.axis_index("gy") & 1).reshape(1).astype(jnp.int32)
    act, dpre, keep, send = forward(codes, core, x, g, zl, zh, yl, yh, kernel)

    plan = exchange_plan()
    first = HALF * C
    sharers = devices // 2
    share = -(-first // (16 * sharers)) * 16
    half_rows = share * sharers
    arrived = swap_with(send, plan[0], 1)
    total = (keep + arrived.astype(F32)).reshape(first, C)
    total = jnp.pad(total, ((0, half_rows - first), (0, 0)))
    done = []

    def ahead(arrived):
        grad = backward(codes, x, dpre, zl, zh, yl, yh, kernel)
        tied = lax.optimization_barrier(tuple(arrived) + (grad,))
        done.append(tied[-1])
        return tied[:-1]

    for level, group in enumerate(plan[1:]):
        total = exchange_sum(total, group, ahead if level == 0 else None)
    scale = 1.0 / (NB * VOX * devices) ** 0.5
    piece = (total * scale).astype(BF16)
    grad_in = done[0]

    pieces = [piece]
    for level, group in enumerate(reversed(plan[1:])):
        if level > 0:
            pieces = [jnp.concatenate(pieces)]
        pieces = [pieces[0]] + [swap_with(pieces[0], group, p) for p in range(1, 1 << len(group))]
    others = [swap_with(p, plan[0], 1) for p in pieces]
    grad_kernel = finish(first, share, plan, pieces + others)
    shape = (1, 1, NB, VOX, C)
    return act.reshape(shape), grad_in.reshape(shape), grad_kernel.reshape(TAPS, C, C)


def solution(mesh):
    placed = (
        P("gz", "gy", None, None, None),
        P("gz", "gy", None),
        P(),
        P("gz", "gy", None, None, None),
    )
    return jax.shard_map(
        local,
        mesh=mesh,
        in_specs=placed,
        out_specs=(P("gz", "gy", None, None, None), P("gz", "gy", None, None, None), P()),
        check_vma=False,
    )
```

```python
import functools

import jax
import jax.numpy as jnp
from jax import lax
from jax.experimental import pallas as pl
from jax.experimental.pallas import tpu as pltpu
from jax.sharding import PartitionSpec as P

C = 128
VOX = 512
BY = 2
BX = 4
NB = 2
SITES = 8
TAPS = 27
HALF = 14

AXES = ("gz", "gy")
F32 = jnp.float32
BF16 = jnp.bfloat16

VZ, VY, VX = 12, 20, 48

SMEM = pl.BlockSpec(memory_space=pltpu.SMEM)
VMEM = pl.BlockSpec(memory_space=pltpu.VMEM)
ANY = pl.BlockSpec(memory_space=pl.ANY)


def exchange_plan():
    gz_bits = [("gz", b) for b in range(lax.axis_size("gz").bit_length() - 1)]
    gy_bits = [("gy", b) for b in range(lax.axis_size("gy").bit_length() - 1)]
    groups, gy_bits = [(gy_bits[0],)], gy_bits[1:]
    while gy_bits and gz_bits:
        groups.append((gy_bits.pop(0), gz_bits.pop(0)))
    rest = gy_bits + gz_bits
    while rest:
        groups.append(tuple(rest[:2]))
        rest = rest[2:]
    return groups


def swap_with(value, group, pattern):
    nz, ny = lax.axis_size("gz"), lax.axis_size("gy")
    flip = {"gz": 0, "gy": 0}
    for k, (axis, bit) in enumerate(group):
        if pattern >> k & 1:
            flip[axis] |= 1 << bit
    pairs = [
        (z * ny + y, (z ^ flip["gz"]) * ny + (y ^ flip["gy"]))
        for z in range(nz)
        for y in range(ny)
    ]
    return lax.ppermute(value, AXES, pairs)


def place_in(group):
    place = jnp.zeros((), jnp.int32)
    for k, (axis, bit) in enumerate(group):
        place = place | (((lax.axis_index(axis) >> bit) & 1) << k)
    return place


def neighbours(up, down, axis):
    count = lax.axis_size(axis)
    forward = [(i, i + 1) for i in range(count - 1)]
    backward = [(b, a) for a, b in forward]
    return lax.ppermute(up, axis, forward), lax.ppermute(down, axis, backward)


Z_ROWS = NB * 24 + 1
Y_ROWS = NB * 24 + 2 * NB * 5 + 3


def pack_z_kernel(sites_ref, x_ref, g_ref, up_ref, down_ref, beside_up, beside_down, sites, sems):
    moves = [(sites_ref, sites)]
    for s in range(NB):
        base = 24 * s
        first, last = slice(base, base + 16), slice(base + 16, base + 24)
        moves += [
            (x_ref.at[s, 6:8], up_ref.at[first].reshape(2, 8, 8, C)),
            (g_ref.at[s, 7], up_ref.at[last]),
            (x_ref.at[s, 0:2], down_ref.at[first].reshape(2, 8, 8, C)),
            (g_ref.at[s, 0], down_ref.at[last]),
            (x_ref.at[s, :, 6:8], beside_up.at[first].reshape(8, 2, 8, C)),
            (g_ref.at[s, :, 7], beside_up.at[last]),
            (x_ref.at[s, :, 0:2], beside_down.at[first].reshape(8, 2, 8, C)),
            (g_ref.at[s, :, 0], beside_down.at[last]),
        ]
    copies = [
        pltpu.make_async_copy(src, dst, sems.at[k]) for k, (src, dst) in enumerate(moves)
    ]
    for copy in copies:
        copy.start()
    copies[0].wait()
    lane = lax.broadcasted_iota(jnp.int32, (8, C), 1)
    code = jnp.zeros((8, C), jnp.int32)
    for s in range(NB):
        code = jnp.where(lane == s, SITES - sites[s], code)
    code = code.astype(F32).astype(BF16)
    up_ref[Z_ROWS - 1] = code
    down_ref[Z_ROWS - 1] = code
    for copy in copies[1:]:
        copy.wait()


def small(limit):
    return pltpu.CompilerParams(vmem_limit_bytes=limit << 20)


def pack_z(sites, x, g):
    shape = jax.ShapeDtypeStruct((Z_ROWS, 8, C), BF16)
    beside = jax.ShapeDtypeStruct((NB * 24, 8, C), BF16)
    return pl.pallas_call(
        pack_z_kernel,
        out_shape=(shape, shape, beside, beside),
        in_specs=[ANY, ANY, ANY],
        out_specs=(VMEM,) * 4,
        scratch_shapes=[pltpu.SMEM((NB,), jnp.int32), pltpu.SemaphoreType.DMA((1 + 8 * NB,))],
        compiler_params=pltpu.CompilerParams(vmem_limit_bytes=67043328),
        name="pack_z",
    )(sites, x, g)


def pack_y_kernel(own_up, own_down, mine_ref, low_ref, high_ref, up_ref, down_ref):
    up_ref[: NB * 24] = own_up[...]
    down_ref[: NB * 24] = own_down[...]
    for side, ref in enumerate((low_ref, high_ref)):
        for s in range(NB):
            base = NB * 24 + 10 * side + 5 * s
            src = 24 * s
            for z in range(2):
                up_ref[base + 2 * z : base + 2 * z + 2] = ref[src + 8 * z + 6 : src + 8 * z + 8]
                down_ref[base + 2 * z : base + 2 * z + 2] = ref[src + 8 * z : src + 8 * z + 2]
            up_ref[base + 4] = ref[src + 16 + 7]
            down_ref[base + 4] = ref[src + 16]
    for k, ref in enumerate((mine_ref, low_ref, high_ref)):
        up_ref[Y_ROWS - 3 + k] = ref[Z_ROWS - 1]
        down_ref[Y_ROWS - 3 + k] = ref[Z_ROWS - 1]


def pack_y(own_up, own_down, mine, low, high):
    shape = jax.ShapeDtypeStruct((Y_ROWS, 8, C), BF16)
    return pl.pallas_call(
        pack_y_kernel,
        out_shape=(shape, shape),
        in_specs=[VMEM] * 5,
        out_specs=(VMEM, VMEM),
        compiler_params=small(4),
        name="pack_y",
    )(own_up, own_down, mine, low, high)


def clear(ref):
    rows = ref.shape[0]
    flat = jnp.zeros((1,) + ref.shape[1:], ref.dtype)
    for z in range(rows):
        ref[z : z + 1] = flat


def place_of(site):
    inside = jnp.minimum(site, SITES - 1)
    return inside // BX, pl.multiple_of(inside % BX * 8 + 8, 8)


def read_codes(sites, zl_ref, zh_ref, yl_ref, yh_ref):
    rows = [zl_ref[Z_ROWS - 1], zh_ref[Z_ROWS - 1]]
    rows += [ref[Y_ROWS - 3 + k] for ref in (yl_ref, yh_ref) for k in range(3)]
    codes = {(0, s): sites[s] for s in range(NB)}
    for k, row in enumerate(rows):
        row = row.astype(F32)
        for s in range(NB):
            codes[k + 1, s] = SITES - row[0, s].astype(jnp.int32)
    return codes


def fill(vol, codes, x_ref, zl_ref, zh_ref, yl_ref, yh_ref):
    def put(z0, y0, x0, rows):
        vol[z0 : z0 + rows.shape[0], pl.ds(y0, rows.shape[1]), pl.ds(x0, 8)] = rows.astype(F32)

    for s in range(NB):
        site = codes[0, s]
        py, px = place_of(site)

        @pl.when(site < SITES)
        def _():
            put(2, 2 + 8 * py, px, x_ref[s])

        for side, ref in ((1, zl_ref), (2, zh_ref)):
            zsite = codes[side, s]
            zpy, zpx = place_of(zsite)

            @pl.when(zsite < SITES)
            def _(ref=ref, side=side, zpy=zpy, zpx=zpx, s=s):
                put(0 if side == 1 else 10, 2 + 8 * zpy, zpx, ref[24 * s : 24 * s + 16].reshape(2, 8, 8, C))

        for first, ref, row, y0 in ((3, yl_ref, 1, 0), (6, yh_ref, 0, 18)):
            for k, (z0, base, depth) in enumerate(
                ((2, 24 * s, 8), (0, 48 + 5 * s, 2), (10, 58 + 5 * s, 2))
            ):
                ysite = codes[first + k, s]
                ypy, ypx = place_of(ysite)

                @pl.when((ysite < SITES) & (ypy == row))
                def _(ref=ref, z0=z0, y0=y0, base=base, depth=depth, ypx=ypx):
                    put(z0, y0, ypx, ref[base : base + 2 * depth].reshape(depth, 2, 8, C))


def stack_x(vol, dst, dst_at, z0, y0s, x0s, nz, ny):
    for z in range(nz):
        for y in range(ny):
            halves = []
            for y0, x0 in zip(y0s, x0s):
                row = vol[z0 + z, y0 + y, pl.ds(x0 - 8, 24)]
                halves.append(
                    jnp.concatenate([row[7:15], row[8:16], row[9:17]], axis=1)
                )
            dst[dst_at + z * ny + y] = jnp.concatenate(halves, axis=0).astype(BF16)


def views(stack, base, ny_all, nz, ny):
    result = []
    for dz in range(3):
        for dy in range(3):
            planes = [
                stack[base + (z + dz) * ny_all + dy : base + (z + dz) * ny_all + dy + ny]
                for z in range(nz)
            ]
            result.append(jnp.concatenate(planes, axis=0).reshape(nz * ny * 16, 3 * C))
    return result


def dot(a, b, dims=((1,), (0,))):
    return lax.dot_general(a, b, (dims, ((), ())), preferred_element_type=F32)


def convolve(stack, base, ny_all, nz, ny, weight):
    total = None
    for k, view in enumerate(views(stack, base, ny_all, nz, ny)):
        term = weight(k, view)
        total = term if total is None else total + term
    return total


def forward_kernel(sites, x_ref, g_ref, zl_ref, zh_ref, yl_ref, yh_ref, w_ref,
                   act_ref, dpre_ref, keep_ref, send_ref, vol, stack, turned, split):
    codes = read_codes(sites, zl_ref, zh_ref, yl_ref, yh_ref)
    core = lax.axis_index("gy") & 1
    clear(vol)
    fill(vol, codes, x_ref, zl_ref, zh_ref, yl_ref, yh_ref)
    places = [place_of(codes[0, s]) for s in range(NB)]
    stack_x(vol, stack, 0, 1, [1 + 8 * py for py, _ in places], [px for _, px in places], 10, 10)

    def weight(k, view):
        return dot(view, w_ref[3 * k : 3 * k + 3].reshape(3 * C, C))

    used = [codes[0, s] < SITES for s in range(NB)]
    for half in range(2):
        pre = convolve(stack, 40 * half, 10, 4, 8, weight)
        sig = 1.0 / (1.0 + jnp.exp(-pre))
        act = (pre * sig).reshape(32, 16, C)
        slope = (sig * (1.0 + pre * (1.0 - sig))).reshape(32, 16, C)
        both = []
        for s in range(NB):
            rows = slice(32 * half, 32 * half + 32)
            a = jnp.where(used[s], act[:, 8 * s : 8 * s + 8], 0.0)
            act_ref[s, rows] = a.astype(BF16)
            d = g_ref[s, 4 * half : 4 * half + 4].astype(F32).reshape(32, 8, C) * slope[:, 8 * s : 8 * s + 8]
            both.append(jnp.where(used[s], d, 0.0))
        d = jnp.concatenate(both, axis=1).astype(BF16)
        dpre_ref[32 * half : 32 * half + 32] = d
        turned[:, 512 * half : 512 * half + 512] = d.reshape(512, C).T

    dt = turned[...]
    for k in range(9):
        dz, dy = divmod(k, 3)
        planes = [stack[(z + dz) * 10 + dy : (z + dz) * 10 + dy + 8] for z in range(8)]
        view = jnp.concatenate(planes, axis=0).reshape(1024, 3 * C)
        term = dot(dt, view)
        for dx in range(3):
            t = 3 * k + dx
            value = term[:, C * dx : C * dx + C].T
            half, at = divmod(t, HALF)
            split[(half ^ core) * HALF + at] = value
    for t in range(TAPS, 2 * HALF):
        half, at = divmod(t, HALF)
        split[(half ^ core) * HALF + at] = jnp.zeros((C, C), F32)
    keep_ref[...] = split[:HALF]
    send_ref[...] = split[HALF:].astype(BF16)


def forward(sites, x, g, zl, zh, yl, yh, w):
    rows = jax.ShapeDtypeStruct((NB, 64, 8, C), BF16)
    return pl.pallas_call(
        forward_kernel,
        out_shape=(
            rows,
            jax.ShapeDtypeStruct((64, 16, C), BF16),
            jax.ShapeDtypeStruct((HALF, C, C), F32),
            jax.ShapeDtypeStruct((HALF, C, C), BF16),
        ),
        in_specs=[SMEM] + [VMEM] * 7,
        out_specs=(VMEM,) * 4,
        scratch_shapes=[
            pltpu.VMEM((VZ, VY, VX, C), F32),
            pltpu.VMEM((100, 16, 3 * C), BF16),
            pltpu.VMEM((C, 1024), BF16),
            pltpu.VMEM((2 * HALF, C, C), F32),
        ],
        compiler_params=small(18),
        cost_estimate=pl.CostEstimate(flops=2 * 10**9, bytes_accessed=5 << 20, transcendentals=1 << 17),
        name="forward",
    )(sites, x, g, zl, zh, yl, yh, w)


def backward_kernel(sites, x_ref, dpre_ref, zl_ref, zh_ref, yl_ref, yh_ref, w_ref,
                    grad_ref, vol, stack):
    codes = read_codes(sites, zl_ref, zh_ref, yl_ref, yh_ref)
    clear(vol)
    fill(vol, codes, x_ref, zl_ref, zh_ref, yl_ref, yh_ref)

    def weight(k, view):
        return dot(view, w_ref[3 * k : 3 * k + 3].reshape(3 * C, C))

    jobs = []
    for block, z in ((1, 1), (2, 10)):
        jobs.append((block, z, None, 1, 8))
    for first, y in ((3, 1), (6, 18)):
        jobs.append((first, 2, y, 8, 1))
        jobs.append((first + 1, 1, y, 1, 1))
        jobs.append((first + 2, 10, y, 1, 1))
    base = 0
    found = []
    for block, z0, y0, nz, ny in jobs:
        places = [place_of(codes[block, s]) for s in range(NB)]
        y0s = [2 + 8 * py if y0 is None else y0 for py, _ in places]
        x0s = [px for _, px in places]
        stack_x(vol, stack, base, z0 - 1, [y - 1 for y in y0s], x0s, nz + 2, ny + 2)
        pre = convolve(stack, base, ny + 2, nz, ny, weight)
        sig = 1.0 / (1.0 + jnp.exp(-pre))
        slope = (sig * (1.0 + pre * (1.0 - sig))).reshape(nz, ny, 16, C)
        found.append((block, z0, y0, nz, ny, y0s, x0s, slope))
        base += (nz + 2) * (ny + 2)
    values = []
    for block, z0, y0, nz, ny, y0s, x0s, slope in found:
        for s in range(NB):
            if block == 1:
                g = zl_ref[24 * s + 16 : 24 * s + 24]
            elif block == 2:
                g = zh_ref[24 * s + 16 : 24 * s + 24]
            else:
                ref = yl_ref if block < 6 else yh_ref
                kind = (block - 3) % 3
                if kind == 0:
                    g = ref[24 * s + 16 : 24 * s + 24]
                else:
                    at = 48 + 10 * (kind - 1) + 5 * s + 4
                    g = ref[at : at + 1]
            g = g.astype(F32).reshape(nz, ny, 8, C)
            value = (g * slope[:, :, 8 * s : 8 * s + 8]).astype(BF16).astype(F32)
            values.append(value)

    clear(vol)
    for s in range(NB):
        site = codes[0, s]
        py, px = place_of(site)

        @pl.when(site < SITES)
        def _(s=s, py=py, px=px):
            own = dpre_ref[...].astype(F32).reshape(8, 8, 16, C)[:, :, 8 * s : 8 * s + 8]
            vol[2:10, pl.ds(2 + 8 * py, 8), pl.ds(px, 8)] = own

    at = 0
    for block, z0, y0, nz, ny, y0s, x0s, slope in found:
        for s in range(NB):
            site = codes[block, s]
            py, px = place_of(site)
            ok = site < SITES
            if block >= 3:
                ok = ok & (py == (1 if block < 6 else 0))
            value = values[at]
            at += 1

            @pl.when(ok)
            def _(value=value, z0=z0, nz=nz, ny=ny, y0=y0s[s], x0=x0s[s]):
                vol[z0 : z0 + nz, pl.ds(y0, ny), pl.ds(x0, 8)] = value

    places = [place_of(codes[0, s]) for s in range(NB)]
    stack_x(vol, stack, 0, 1, [1 + 8 * py for py, _ in places], [px for _, px in places], 10, 10)

    def back(k, view):
        turned = [w_ref[26 - 3 * k - dx] for dx in range(3)]
        return dot(view, jnp.concatenate(turned, axis=1), ((1,), (1,)))

    for half in range(2):
        grad = convolve(stack, 40 * half, 10, 4, 8, back).reshape(32, 16, C)
        for s in range(NB):
            value = jnp.where(codes[0, s] < SITES, grad[:, 8 * s : 8 * s + 8], 0.0)
            grad_ref[s, 32 * half : 32 * half + 32] = value.astype(BF16)


def backward(sites, x, dpre, zl, zh, yl, yh, w):
    return pl.pallas_call(
        backward_kernel,
        out_shape=jax.ShapeDtypeStruct((NB, 64, 8, C), BF16),
        in_specs=[SMEM] + [VMEM] * 7,
        out_specs=VMEM,
        scratch_shapes=[
            pltpu.VMEM((VZ, VY, VX, C), F32),
            pltpu.VMEM((160, 16, 3 * C), BF16),
        ],
        compiler_params=small(18),
        cost_estimate=pl.CostEstimate(flops=10**9, bytes_accessed=5 << 20, transcendentals=1 << 16),
        name="backward",
    )(sites, x, dpre, zl, zh, yl, yh, w)


def merge_kernel(group, scale, count, *refs):
    terms, outs = refs[:count], refs[count:]
    rows = outs[0].shape[0]
    me = place_in(group) if group else 0
    for p, out in enumerate(outs):
        at = pl.multiple_of((me ^ p) * rows, 16) if group else 0
        value = terms[0][pl.ds(at, rows)]
        for term in terms[1:]:
            value = value + term[pl.ds(at, rows)].astype(F32)
        out[...] = value if group and p == 0 else (value * scale).astype(BF16)


def merge(keep, arrived, group=None, scale=1.0):
    members = 1 << len(group) if group else 1
    shape = (keep.shape[0] // members, C)
    kinds = [F32] + [BF16] * (members - 1) if group else [BF16]
    return pl.pallas_call(
        functools.partial(merge_kernel, group, scale, 1 + len(arrived)),
        out_shape=tuple(jax.ShapeDtypeStruct(shape, kind) for kind in kinds),
        in_specs=[VMEM] * (1 + len(arrived)),
        out_specs=(VMEM,) * members,
        compiler_params=small(6),
        name="merge",
    )(keep, *arrived)


def join_kernel(*refs):
    out = refs[-1]
    for k, ref in enumerate(refs[:-1]):
        out[k * ref.shape[0] : (k + 1) * ref.shape[0]] = ref[...]


def join(pieces):
    rows = sum(p.shape[0] for p in pieces)
    return pl.pallas_call(
        join_kernel,
        out_shape=jax.ShapeDtypeStruct((rows, C), BF16),
        in_specs=[VMEM] * len(pieces),
        out_specs=VMEM,
        compiler_params=small(4),
        name="join",
    )(*pieces)


def finish_kernel(first, share, plan, *refs):
    pieces, out = refs[:-1], refs[-1]
    me = [place_in(group) for group in plan]
    sizes = [1 << len(group) for group in plan]
    middle, inner_sizes = sizes[1], sizes[2:]
    inner = 1
    for n in inner_sizes:
        inner *= n
    for k, ref in enumerate(pieces):
        half = (k // middle) ^ me[0]
        outer = (k % middle) ^ me[1]
        for r in range(inner):
            block, stride, rest = outer * inner, inner, r
            for level, n in enumerate(inner_sizes):
                stride //= n
                digit, rest = divmod(rest, stride)
                block = block + (digit ^ me[2 + level]) * stride
            value = ref[r * share : (r + 1) * share].astype(F32)
            for h in range(2):
                whole, rem = divmod(min(first, TAPS * C - h * first), share)

                @pl.when((half == h) & (block < whole))
                def _(value=value, h=h, block=block):
                    out[pl.ds(pl.multiple_of(h * first + block * share, 8), share)] = value

                if rem:

                    @pl.when((half == h) & (block == whole))
                    def _(value=value, h=h, whole=whole, rem=rem):
                        at = h * first + whole * share
                        out[at : at + rem] = value[:rem]


def finish(first, share, plan, pieces):
    return pl.pallas_call(
        functools.partial(finish_kernel, first, share, plan),
        out_shape=jax.ShapeDtypeStruct((TAPS * C, C), F32),
        in_specs=[VMEM] * len(pieces),
        out_specs=VMEM,
        compiler_params=small(8),
        name="finish",
    )(*pieces)


def local(features, brick_sites, kernel, cotangent):
    x = features.reshape(NB, 8, 8, 8, C)
    g = cotangent.reshape(NB, 8, 8, 8, C)
    sites = brick_sites.reshape(NB)
    devices = lax.axis_size("gz") * lax.axis_size("gy")
    z_up, z_down, own_up, own_down = pack_z(sites, x, g)
    zl, zh = neighbours(z_up, z_down, "gz")
    y_up, y_down = pack_y(own_up, own_down, z_up, zl, zh)
    yl, yh = neighbours(y_up, y_down, "gy")
    act, dpre, keep, send = forward(sites, x, g, zl, zh, yl, yh, kernel)

    plan = exchange_plan()
    first = HALF * C
    sharers = devices // 2
    share = -(-first // (16 * sharers)) * 16
    half_rows = share * sharers
    arrived = swap_with(send, plan[0], 1)
    pad = ((0, half_rows - first), (0, 0))
    keep = jnp.pad(keep.reshape(first, C), pad)
    arrived = jnp.pad(arrived.reshape(first, C), pad)
    grad_in = None
    arrived = [arrived]
    for group in plan[1:]:
        keep, *sends = merge(keep, arrived, group)
        arrived = [swap_with(send, group, 1 + k) for k, send in enumerate(sends)]
        if grad_in is None:
            grad_in = backward(sites, x, dpre, zl, zh, yl, yh, kernel)
            *arrived, grad_in = lax.optimization_barrier((*arrived, grad_in))
    (piece,) = merge(keep, arrived, scale=1.0 / (NB * VOX * devices) ** 0.5)

    pieces = [piece]
    for level, group in enumerate(reversed(plan[1:])):
        if level > 0:
            pieces = [join(pieces)]
        pieces = [pieces[0]] + [swap_with(pieces[0], group, p) for p in range(1, 1 << len(group))]
    others = [swap_with(p, plan[0], 1) for p in pieces]
    grad_kernel = finish(first, share, plan, pieces + others)
    shape = (1, 1, NB, VOX, C)
    return act.reshape(shape), grad_in.reshape(shape), grad_kernel.reshape(TAPS, C, C)


def solution(mesh):
    placed = (
        P("gz", "gy", None, None, None),
        P("gz", "gy", None),
        P(),
        P("gz", "gy", None, None, None),
    )
    return jax.shard_map(
        local,
        mesh=mesh,
        in_specs=placed,
        out_specs=(P("gz", "gy", None, None, None), P("gz", "gy", None, None, None), P()),
        check_vma=False,
    )
```

```python
import functools

import jax
import jax.numpy as jnp
from jax import lax
from jax.experimental import pallas as pl
from jax.experimental.pallas import tpu as pltpu
from jax.sharding import PartitionSpec as P

C = 128
VOX = 512
BY = 2
BX = 4
NB = 2
SITES = 8
TAPS = 27
HALF = 14

AXES = ("gz", "gy")
F32 = jnp.float32
BF16 = jnp.bfloat16

VZ, VY, VX = 12, 20, 48

SMEM = pl.BlockSpec(memory_space=pltpu.SMEM)
VMEM = pl.BlockSpec(memory_space=pltpu.VMEM)
ANY = pl.BlockSpec(memory_space=pl.ANY)


def exchange_plan():
    gz_bits = [("gz", b) for b in range(lax.axis_size("gz").bit_length() - 1)]
    gy_bits = [("gy", b) for b in range(lax.axis_size("gy").bit_length() - 1)]
    groups, gy_bits = [(gy_bits[0],)], gy_bits[1:]
    while gy_bits and gz_bits:
        groups.append((gy_bits.pop(0), gz_bits.pop(0)))
    rest = gy_bits + gz_bits
    while rest:
        groups.append(tuple(rest[:2]))
        rest = rest[2:]
    return groups


def swap_with(value, group, pattern):
    nz, ny = lax.axis_size("gz"), lax.axis_size("gy")
    flip = {"gz": 0, "gy": 0}
    for k, (axis, bit) in enumerate(group):
        if pattern >> k & 1:
            flip[axis] |= 1 << bit
    pairs = [
        (z * ny + y, (z ^ flip["gz"]) * ny + (y ^ flip["gy"]))
        for z in range(nz)
        for y in range(ny)
    ]
    return lax.ppermute(value, AXES, pairs)


def place_in(group):
    place = jnp.zeros((), jnp.int32)
    for k, (axis, bit) in enumerate(group):
        place = place | (((lax.axis_index(axis) >> bit) & 1) << k)
    return place


def neighbours(up, down, axis):
    count = lax.axis_size(axis)
    forward = [(i, i + 1) for i in range(count - 1)]
    backward = [(b, a) for a, b in forward]
    return lax.ppermute(up, axis, forward), lax.ppermute(down, axis, backward)


Z_ROWS = NB * 24 + 1
Y_ROWS = NB * 24 + 2 * NB * 5 + 3


def code_row(sites):
    lane = lax.broadcasted_iota(jnp.int32, (8, C), 1)
    code = jnp.zeros((8, C), jnp.int32)
    for s in range(NB):
        code = jnp.where(lane == s, SITES - sites[s], code)
    return code.astype(F32).astype(BF16)


def pack_z_kernel(sites_ref, x_ref, g_ref, up_ref, down_ref, sites, sems):
    moves = [(sites_ref, sites)]
    for s in range(NB):
        base = 24 * s
        first, last = slice(base, base + 16), slice(base + 16, base + 24)
        moves += [
            (x_ref.at[s, 6:8], up_ref.at[first].reshape(2, 8, 8, C)),
            (g_ref.at[s, 7], up_ref.at[last]),
            (x_ref.at[s, 0:2], down_ref.at[first].reshape(2, 8, 8, C)),
            (g_ref.at[s, 0], down_ref.at[last]),
        ]
    copies = [
        pltpu.make_async_copy(src, dst, sems.at[k]) for k, (src, dst) in enumerate(moves)
    ]
    for copy in copies:
        copy.start()
    copies[0].wait()
    code = code_row(sites)
    up_ref[Z_ROWS - 1] = code
    down_ref[Z_ROWS - 1] = code
    for copy in copies[1:]:
        copy.wait()


def small(limit):
    return pltpu.CompilerParams(vmem_limit_bytes=limit << 20)


def pack_z(sites, x, g):
    shape = jax.ShapeDtypeStruct((Z_ROWS, 8, C), BF16)
    return pl.pallas_call(
        pack_z_kernel,
        out_shape=(shape, shape),
        in_specs=[ANY, ANY, ANY],
        out_specs=(VMEM,) * 2,
        scratch_shapes=[pltpu.SMEM((NB,), jnp.int32), pltpu.SemaphoreType.DMA((1 + 4 * NB,))],
        compiler_params=pltpu.CompilerParams(vmem_limit_bytes=67043328),
        name="pack_z",
    )(sites, x, g)


def stage_kernel(sites, x_ref, g_ref, w_ref, x_out, g_out, w_out, code_out, up_ref, down_ref):
    x_out[...] = x_ref[...]
    g_out[...] = g_ref[...]
    w_out[...] = w_ref[...]
    code_out[0] = code_row(sites)
    for s in range(NB):
        first, last = slice(24 * s, 24 * s + 16), slice(24 * s + 16, 24 * s + 24)
        up_ref[first] = x_ref[s, :, 6:8].reshape(16, 8, C)
        up_ref[last] = g_ref[s, :, 7]
        down_ref[first] = x_ref[s, :, 0:2].reshape(16, 8, C)
        down_ref[last] = g_ref[s, :, 0]


def stage(sites, x, g, w):
    beside = jax.ShapeDtypeStruct((NB * 24, 8, C), BF16)
    code = jax.ShapeDtypeStruct((1, 8, C), BF16)
    kept = tuple(jax.ShapeDtypeStruct(a.shape, a.dtype) for a in (x, g, w))
    return pl.pallas_call(
        stage_kernel,
        out_shape=kept + (code, beside, beside),
        in_specs=[SMEM, VMEM, VMEM, VMEM],
        out_specs=(VMEM,) * 6,
        compiler_params=small(4),
        name="stage",
    )(sites, x, g, w)


def pack_y_kernel(own_up, own_down, mine_ref, low_ref, high_ref, up_ref, down_ref):
    up_ref[: NB * 24] = own_up[...]
    down_ref[: NB * 24] = own_down[...]
    for side, ref in enumerate((low_ref, high_ref)):
        for s in range(NB):
            base = NB * 24 + 10 * side + 5 * s
            src = 24 * s
            for z in range(2):
                up_ref[base + 2 * z : base + 2 * z + 2] = ref[src + 8 * z + 6 : src + 8 * z + 8]
                down_ref[base + 2 * z : base + 2 * z + 2] = ref[src + 8 * z : src + 8 * z + 2]
            up_ref[base + 4] = ref[src + 16 + 7]
            down_ref[base + 4] = ref[src + 16]
    for k, row in enumerate((mine_ref[0], low_ref[Z_ROWS - 1], high_ref[Z_ROWS - 1])):
        up_ref[Y_ROWS - 3 + k] = row
        down_ref[Y_ROWS - 3 + k] = row


def pack_y(own_up, own_down, mine, low, high):
    shape = jax.ShapeDtypeStruct((Y_ROWS, 8, C), BF16)
    return pl.pallas_call(
        pack_y_kernel,
        out_shape=(shape, shape),
        in_specs=[VMEM] * 5,
        out_specs=(VMEM, VMEM),
        compiler_params=small(4),
        name="pack_y",
    )(own_up, own_down, mine, low, high)


def clear(ref):
    rows = ref.shape[0]
    flat = jnp.zeros((1,) + ref.shape[1:], ref.dtype)
    for z in range(rows):
        ref[z : z + 1] = flat


def place_of(site):
    inside = jnp.minimum(site, SITES - 1)
    return inside // BX, pl.multiple_of(inside % BX * 8 + 8, 8)


def read_codes(mine_ref, zl_ref, zh_ref, yl_ref, yh_ref):
    rows = [mine_ref[0], zl_ref[Z_ROWS - 1], zh_ref[Z_ROWS - 1]]
    rows += [ref[Y_ROWS - 3 + k] for ref in (yl_ref, yh_ref) for k in range(3)]
    codes = {}
    for k, row in enumerate(rows):
        row = row.astype(F32)
        for s in range(NB):
            codes[k, s] = SITES - row[0, s].astype(jnp.int32)
    return codes


def fill(vol, codes, x_ref, zl_ref, zh_ref, yl_ref, yh_ref):
    def put(z0, y0, x0, rows):
        vol[z0 : z0 + rows.shape[0], pl.ds(y0, rows.shape[1]), pl.ds(x0, 8)] = rows.astype(F32)

    for s in range(NB):
        site = codes[0, s]
        py, px = place_of(site)

        @pl.when(site < SITES)
        def _():
            put(2, 2 + 8 * py, px, x_ref[s])

        for side, ref in ((1, zl_ref), (2, zh_ref)):
            zsite = codes[side, s]
            zpy, zpx = place_of(zsite)

            @pl.when(zsite < SITES)
            def _(ref=ref, side=side, zpy=zpy, zpx=zpx, s=s):
                put(0 if side == 1 else 10, 2 + 8 * zpy, zpx, ref[24 * s : 24 * s + 16].reshape(2, 8, 8, C))

        for first, ref, row, y0 in ((3, yl_ref, 1, 0), (6, yh_ref, 0, 18)):
            for k, (z0, base, depth) in enumerate(
                ((2, 24 * s, 8), (0, 48 + 5 * s, 2), (10, 58 + 5 * s, 2))
            ):
                ysite = codes[first + k, s]
                ypy, ypx = place_of(ysite)

                @pl.when((ysite < SITES) & (ypy == row))
                def _(ref=ref, z0=z0, y0=y0, base=base, depth=depth, ypx=ypx):
                    put(z0, y0, ypx, ref[base : base + 2 * depth].reshape(depth, 2, 8, C))


def stack_x(vol, dst, dst_at, z0, y0s, x0s, nz, ny):
    for z in range(nz):
        for y in range(ny):
            halves = []
            for y0, x0 in zip(y0s, x0s):
                row = vol[z0 + z, y0 + y, pl.ds(x0 - 8, 24)]
                halves.append(
                    jnp.concatenate([row[7:15], row[8:16], row[9:17]], axis=1)
                )
            dst[dst_at + z * ny + y] = jnp.concatenate(halves, axis=0).astype(BF16)


def views(stack, base, ny_all, nz, ny):
    result = []
    for dz in range(3):
        for dy in range(3):
            planes = [
                stack[base + (z + dz) * ny_all + dy : base + (z + dz) * ny_all + dy + ny]
                for z in range(nz)
            ]
            result.append(jnp.concatenate(planes, axis=0).reshape(nz * ny * 16, 3 * C))
    return result


def dot(a, b, dims=((1,), (0,))):
    return lax.dot_general(a, b, (dims, ((), ())), preferred_element_type=F32)


def convolve(stack, base, ny_all, nz, ny, weight):
    total = None
    for k, view in enumerate(views(stack, base, ny_all, nz, ny)):
        term = weight(k, view)
        total = term if total is None else total + term
    return total


def forward_kernel(mine_ref, x_ref, g_ref, zl_ref, zh_ref, yl_ref, yh_ref, w_ref,
                   act_ref, dpre_ref, keep_ref, send_ref, vol, stack, turned, split):
    codes = read_codes(mine_ref, zl_ref, zh_ref, yl_ref, yh_ref)
    core = lax.axis_index("gy") & 1
    clear(vol)
    fill(vol, codes, x_ref, zl_ref, zh_ref, yl_ref, yh_ref)
    places = [place_of(codes[0, s]) for s in range(NB)]
    stack_x(vol, stack, 0, 1, [1 + 8 * py for py, _ in places], [px for _, px in places], 10, 10)

    def weight(k, view):
        return dot(view, w_ref[3 * k : 3 * k + 3].reshape(3 * C, C))

    used = [codes[0, s] < SITES for s in range(NB)]
    for half in range(2):
        pre = convolve(stack, 40 * half, 10, 4, 8, weight)
        sig = 1.0 / (1.0 + jnp.exp(-pre))
        act = (pre * sig).reshape(32, 16, C)
        slope = (sig * (1.0 + pre * (1.0 - sig))).reshape(32, 16, C)
        both = []
        for s in range(NB):
            rows = slice(32 * half, 32 * half + 32)
            a = jnp.where(used[s], act[:, 8 * s : 8 * s + 8], 0.0)
            act_ref[s, rows] = a.astype(BF16)
            d = g_ref[s, 4 * half : 4 * half + 4].astype(F32).reshape(32, 8, C) * slope[:, 8 * s : 8 * s + 8]
            both.append(jnp.where(used[s], d, 0.0))
        d = jnp.concatenate(both, axis=1).astype(BF16)
        dpre_ref[32 * half : 32 * half + 32] = d
        turned[:, 512 * half : 512 * half + 512] = d.reshape(512, C).T

    dt = turned[...]
    for k in range(9):
        dz, dy = divmod(k, 3)
        planes = [stack[(z + dz) * 10 + dy : (z + dz) * 10 + dy + 8] for z in range(8)]
        view = jnp.concatenate(planes, axis=0).reshape(1024, 3 * C)
        term = dot(dt, view)
        for dx in range(3):
            t = 3 * k + dx
            value = term[:, C * dx : C * dx + C].T
            half, at = divmod(t, HALF)
            split[(half ^ core) * HALF + at] = value
    for t in range(TAPS, 2 * HALF):
        half, at = divmod(t, HALF)
        split[(half ^ core) * HALF + at] = jnp.zeros((C, C), F32)
    keep_ref[...] = split[:HALF]
    send_ref[...] = split[HALF:].astype(BF16)


def forward(sites, x, g, zl, zh, yl, yh, w):
    rows = jax.ShapeDtypeStruct((NB, 64, 8, C), BF16)
    return pl.pallas_call(
        forward_kernel,
        out_shape=(
            rows,
            jax.ShapeDtypeStruct((64, 16, C), BF16),
            jax.ShapeDtypeStruct((HALF, C, C), F32),
            jax.ShapeDtypeStruct((HALF, C, C), BF16),
        ),
        in_specs=[VMEM] * 8,
        out_specs=(VMEM,) * 4,
        scratch_shapes=[
            pltpu.VMEM((VZ, VY, VX, C), F32),
            pltpu.VMEM((100, 16, 3 * C), BF16),
            pltpu.VMEM((C, 1024), BF16),
            pltpu.VMEM((2 * HALF, C, C), F32),
        ],
        compiler_params=small(18),
        cost_estimate=pl.CostEstimate(flops=2 * 10**9, bytes_accessed=5 << 20, transcendentals=1 << 17),
        name="forward",
    )(sites, x, g, zl, zh, yl, yh, w)


def backward_kernel(mine_ref, x_ref, dpre_ref, zl_ref, zh_ref, yl_ref, yh_ref, w_ref,
                    grad_ref, vol, stack):
    codes = read_codes(mine_ref, zl_ref, zh_ref, yl_ref, yh_ref)
    clear(vol)
    fill(vol, codes, x_ref, zl_ref, zh_ref, yl_ref, yh_ref)

    def weight(k, view):
        return dot(view, w_ref[3 * k : 3 * k + 3].reshape(3 * C, C))

    jobs = []
    for block, z in ((1, 1), (2, 10)):
        jobs.append((block, z, None, 1, 8))
    for first, y in ((3, 1), (6, 18)):
        jobs.append((first, 2, y, 8, 1))
        jobs.append((first + 1, 1, y, 1, 1))
        jobs.append((first + 2, 10, y, 1, 1))
    base = 0
    found = []
    for block, z0, y0, nz, ny in jobs:
        places = [place_of(codes[block, s]) for s in range(NB)]
        y0s = [2 + 8 * py if y0 is None else y0 for py, _ in places]
        x0s = [px for _, px in places]
        stack_x(vol, stack, base, z0 - 1, [y - 1 for y in y0s], x0s, nz + 2, ny + 2)
        pre = convolve(stack, base, ny + 2, nz, ny, weight)
        sig = 1.0 / (1.0 + jnp.exp(-pre))
        slope = (sig * (1.0 + pre * (1.0 - sig))).reshape(nz, ny, 16, C)
        found.append((block, z0, y0, nz, ny, y0s, x0s, slope))
        base += (nz + 2) * (ny + 2)
    values = []
    for block, z0, y0, nz, ny, y0s, x0s, slope in found:
        for s in range(NB):
            if block == 1:
                g = zl_ref[24 * s + 16 : 24 * s + 24]
            elif block == 2:
                g = zh_ref[24 * s + 16 : 24 * s + 24]
            else:
                ref = yl_ref if block < 6 else yh_ref
                kind = (block - 3) % 3
                if kind == 0:
                    g = ref[24 * s + 16 : 24 * s + 24]
                else:
                    at = 48 + 10 * (kind - 1) + 5 * s + 4
                    g = ref[at : at + 1]
            g = g.astype(F32).reshape(nz, ny, 8, C)
            value = (g * slope[:, :, 8 * s : 8 * s + 8]).astype(BF16).astype(F32)
            values.append(value)

    clear(vol)
    for s in range(NB):
        site = codes[0, s]
        py, px = place_of(site)

        @pl.when(site < SITES)
        def _(s=s, py=py, px=px):
            own = dpre_ref[...].astype(F32).reshape(8, 8, 16, C)[:, :, 8 * s : 8 * s + 8]
            vol[2:10, pl.ds(2 + 8 * py, 8), pl.ds(px, 8)] = own

    at = 0
    for block, z0, y0, nz, ny, y0s, x0s, slope in found:
        for s in range(NB):
            site = codes[block, s]
            py, px = place_of(site)
            ok = site < SITES
            if block >= 3:
                ok = ok & (py == (1 if block < 6 else 0))
            value = values[at]
            at += 1

            @pl.when(ok)
            def _(value=value, z0=z0, nz=nz, ny=ny, y0=y0s[s], x0=x0s[s]):
                vol[z0 : z0 + nz, pl.ds(y0, ny), pl.ds(x0, 8)] = value

    places = [place_of(codes[0, s]) for s in range(NB)]
    stack_x(vol, stack, 0, 1, [1 + 8 * py for py, _ in places], [px for _, px in places], 10, 10)

    def back(k, view):
        turned = [w_ref[26 - 3 * k - dx] for dx in range(3)]
        return dot(view, jnp.concatenate(turned, axis=1), ((1,), (1,)))

    for half in range(2):
        grad = convolve(stack, 40 * half, 10, 4, 8, back).reshape(32, 16, C)
        for s in range(NB):
            value = jnp.where(codes[0, s] < SITES, grad[:, 8 * s : 8 * s + 8], 0.0)
            grad_ref[s, 32 * half : 32 * half + 32] = value.astype(BF16)


def backward(sites, x, dpre, zl, zh, yl, yh, w):
    return pl.pallas_call(
        backward_kernel,
        out_shape=jax.ShapeDtypeStruct((NB, 64, 8, C), BF16),
        in_specs=[VMEM] * 8,
        out_specs=VMEM,
        scratch_shapes=[
            pltpu.VMEM((VZ, VY, VX, C), F32),
            pltpu.VMEM((160, 16, 3 * C), BF16),
        ],
        compiler_params=small(18),
        cost_estimate=pl.CostEstimate(flops=10**9, bytes_accessed=5 << 20, transcendentals=1 << 16),
        name="backward",
    )(sites, x, dpre, zl, zh, yl, yh, w)


def merge_kernel(group, scale, count, *refs):
    terms, outs = refs[:count], refs[count:]
    rows = outs[0].shape[0]
    me = place_in(group) if group else 0
    for p, out in enumerate(outs):
        at = pl.multiple_of((me ^ p) * rows, 16) if group else 0
        value = terms[0][pl.ds(at, rows)]
        for term in terms[1:]:
            value = value + term[pl.ds(at, rows)].astype(F32)
        out[...] = value if group and p == 0 else (value * scale).astype(BF16)


def merge(keep, arrived, group=None, scale=1.0):
    members = 1 << len(group) if group else 1
    shape = (keep.shape[0] // members, C)
    kinds = [F32] + [BF16] * (members - 1) if group else [BF16]
    return pl.pallas_call(
        functools.partial(merge_kernel, group, scale, 1 + len(arrived)),
        out_shape=tuple(jax.ShapeDtypeStruct(shape, kind) for kind in kinds),
        in_specs=[VMEM] * (1 + len(arrived)),
        out_specs=(VMEM,) * members,
        compiler_params=small(6),
        name="merge",
    )(keep, *arrived)


def join_kernel(*refs):
    out = refs[-1]
    for k, ref in enumerate(refs[:-1]):
        out[k * ref.shape[0] : (k + 1) * ref.shape[0]] = ref[...]


def join(pieces):
    rows = sum(p.shape[0] for p in pieces)
    return pl.pallas_call(
        join_kernel,
        out_shape=jax.ShapeDtypeStruct((rows, C), BF16),
        in_specs=[VMEM] * len(pieces),
        out_specs=VMEM,
        compiler_params=small(4),
        name="join",
    )(*pieces)


def finish_kernel(first, share, plan, *refs):
    pieces, out = refs[:-1], refs[-1]
    me = [place_in(group) for group in plan]
    sizes = [1 << len(group) for group in plan]
    middle, inner_sizes = sizes[1], sizes[2:]
    inner = 1
    for n in inner_sizes:
        inner *= n
    for k, ref in enumerate(pieces):
        half = (k // middle) ^ me[0]
        outer = (k % middle) ^ me[1]
        for r in range(inner):
            block, stride, rest = outer * inner, inner, r
            for level, n in enumerate(inner_sizes):
                stride //= n
                digit, rest = divmod(rest, stride)
                block = block + (digit ^ me[2 + level]) * stride
            value = ref[r * share : (r + 1) * share].astype(F32)
            for h in range(2):
                whole, rem = divmod(min(first, TAPS * C - h * first), share)

                @pl.when((half == h) & (block < whole))
                def _(value=value, h=h, block=block):
                    out[pl.ds(pl.multiple_of(h * first + block * share, 8), share)] = value

                if rem:

                    @pl.when((half == h) & (block == whole))
                    def _(value=value, h=h, whole=whole, rem=rem):
                        at = h * first + whole * share
                        out[at : at + rem] = value[:rem]


def finish(first, share, plan, pieces):
    return pl.pallas_call(
        functools.partial(finish_kernel, first, share, plan),
        out_shape=jax.ShapeDtypeStruct((TAPS * C, C), F32),
        in_specs=[VMEM] * len(pieces),
        out_specs=VMEM,
        compiler_params=small(8),
        name="finish",
    )(*pieces)


def local(features, brick_sites, kernel, cotangent):
    x = features.reshape(NB, 8, 8, 8, C)
    g = cotangent.reshape(NB, 8, 8, 8, C)
    sites = brick_sites.reshape(NB)
    devices = lax.axis_size("gz") * lax.axis_size("gy")
    z_up, z_down = pack_z(sites, x, g)
    z_up, z_down, *later = lax.optimization_barrier((z_up, z_down, sites, x, g, kernel))
    x, g, w, mine, own_up, own_down = stage(*later)
    zl, zh = neighbours(z_up, z_down, "gz")
    y_up, y_down = pack_y(own_up, own_down, mine, zl, zh)
    yl, yh = neighbours(y_up, y_down, "gy")
    act, dpre, keep, send = forward(mine, x, g, zl, zh, yl, yh, w)

    plan = exchange_plan()
    first = HALF * C
    sharers = devices // 2
    share = -(-first // (16 * sharers)) * 16
    half_rows = share * sharers
    arrived = swap_with(send, plan[0], 1)
    pad = ((0, half_rows - first), (0, 0))
    keep = jnp.pad(keep.reshape(first, C), pad)
    arrived = jnp.pad(arrived.reshape(first, C), pad)
    grad_in = None
    arrived = [arrived]
    for group in plan[1:]:
        keep, *sends = merge(keep, arrived, group)
        arrived = [swap_with(send, group, 1 + k) for k, send in enumerate(sends)]
        if grad_in is None:
            grad_in = backward(mine, x, dpre, zl, zh, yl, yh, w)
            *arrived, grad_in = lax.optimization_barrier((*arrived, grad_in))
    (piece,) = merge(keep, arrived, scale=1.0 / (NB * VOX * devices) ** 0.5)

    pieces = [piece]
    for level, group in enumerate(reversed(plan[1:])):
        if level > 0:
            pieces = [join(pieces)]
        pieces = [pieces[0]] + [swap_with(pieces[0], group, p) for p in range(1, 1 << len(group))]
    others = [swap_with(p, plan[0], 1) for p in pieces]
    grad_kernel = finish(first, share, plan, pieces + others)
    shape = (1, 1, NB, VOX, C)
    return act.reshape(shape), grad_in.reshape(shape), grad_kernel.reshape(TAPS, C, C)


def solution(mesh):
    placed = (
        P("gz", "gy", None, None, None),
        P("gz", "gy", None),
        P(),
        P("gz", "gy", None, None, None),
    )
    return jax.shard_map(
        local,
        mesh=mesh,
        in_specs=placed,
        out_specs=(P("gz", "gy", None, None, None), P("gz", "gy", None, None, None), P()),
        check_vma=False,
    )
```

```python
import functools

import jax
import jax.numpy as jnp
from jax import lax
from jax.experimental import pallas as pl
from jax.experimental.pallas import tpu as pltpu
from jax.sharding import PartitionSpec as P

C = 128
VOX = 512
BY = 2
BX = 4
NB = 2
SITES = 8
TAPS = 27
HALF = 14

AXES = ("gz", "gy")
F32 = jnp.float32
BF16 = jnp.bfloat16

VZ, VY, VX = 12, 20, 48

SMEM = pl.BlockSpec(memory_space=pltpu.SMEM)
VMEM = pl.BlockSpec(memory_space=pltpu.VMEM)
ANY = pl.BlockSpec(memory_space=pl.ANY)


def exchange_plan():
    gz_bits = [("gz", b) for b in range(lax.axis_size("gz").bit_length() - 1)]
    gy_bits = [("gy", b) for b in range(lax.axis_size("gy").bit_length() - 1)]
    groups, gy_bits = [(gy_bits[0],)], gy_bits[1:]
    while gy_bits and gz_bits:
        groups.append((gy_bits.pop(0), gz_bits.pop(0)))
    rest = gy_bits + gz_bits
    while rest:
        groups.append((rest.pop(0),))
    return groups


def swap_with(value, group, pattern):
    nz, ny = lax.axis_size("gz"), lax.axis_size("gy")
    flip = {"gz": 0, "gy": 0}
    for k, (axis, bit) in enumerate(group):
        if pattern >> k & 1:
            flip[axis] |= 1 << bit
    pairs = [
        (z * ny + y, (z ^ flip["gz"]) * ny + (y ^ flip["gy"]))
        for z in range(nz)
        for y in range(ny)
    ]
    return lax.ppermute(value, AXES, pairs)


def place_in(group):
    place = jnp.zeros((), jnp.int32)
    for k, (axis, bit) in enumerate(group):
        place = place | (((lax.axis_index(axis) >> bit) & 1) << k)
    return place


def neighbours(up, down, axis):
    count = lax.axis_size(axis)
    forward = [(i, i + 1) for i in range(count - 1)]
    backward = [(b, a) for a, b in forward]
    return lax.ppermute(up, axis, forward), lax.ppermute(down, axis, backward)


Z_ROWS = NB * 24 + 1
Y_ROWS = NB * 24 + 2 * NB * 5 + 3


def code_row(sites):
    lane = lax.broadcasted_iota(jnp.int32, (8, C), 1)
    code = jnp.zeros((8, C), jnp.int32)
    for s in range(NB):
        code = jnp.where(lane == s, SITES - sites[s], code)
    return code.astype(F32).astype(BF16)


def pack_z_kernel(sites_ref, x_ref, g_ref, up_ref, down_ref, sites, sems):
    moves = [(sites_ref, sites)]
    for s in range(NB):
        base = 24 * s
        first, last = slice(base, base + 16), slice(base + 16, base + 24)
        moves += [
            (x_ref.at[s, 6:8], up_ref.at[first].reshape(2, 8, 8, C)),
            (g_ref.at[s, 7], up_ref.at[last]),
            (x_ref.at[s, 0:2], down_ref.at[first].reshape(2, 8, 8, C)),
            (g_ref.at[s, 0], down_ref.at[last]),
        ]
    copies = [
        pltpu.make_async_copy(src, dst, sems.at[k]) for k, (src, dst) in enumerate(moves)
    ]
    for copy in copies:
        copy.start()
    copies[0].wait()
    code = code_row(sites)
    up_ref[Z_ROWS - 1] = code
    down_ref[Z_ROWS - 1] = code
    for copy in copies[1:]:
        copy.wait()


def small(limit):
    return pltpu.CompilerParams(vmem_limit_bytes=limit << 20)


def pack_z(sites, x, g):
    shape = jax.ShapeDtypeStruct((Z_ROWS, 8, C), BF16)
    return pl.pallas_call(
        pack_z_kernel,
        out_shape=(shape, shape),
        in_specs=[ANY, ANY, ANY],
        out_specs=(VMEM,) * 2,
        scratch_shapes=[pltpu.SMEM((NB,), jnp.int32), pltpu.SemaphoreType.DMA((1 + 4 * NB,))],
        compiler_params=pltpu.CompilerParams(vmem_limit_bytes=67043328),
        name="pack_z",
    )(sites, x, g)


def stage_kernel(sites, x_ref, g_ref, w_ref, x_out, g_out, w_out, code_out, up_ref, down_ref):
    x_out[...] = x_ref[...]
    g_out[...] = g_ref[...]
    w_out[...] = w_ref[...]
    code_out[0] = code_row(sites)
    for s in range(NB):
        first, last = slice(24 * s, 24 * s + 16), slice(24 * s + 16, 24 * s + 24)
        up_ref[first] = x_ref[s, :, 6:8].reshape(16, 8, C)
        up_ref[last] = g_ref[s, :, 7]
        down_ref[first] = x_ref[s, :, 0:2].reshape(16, 8, C)
        down_ref[last] = g_ref[s, :, 0]


def stage(sites, x, g, w):
    beside = jax.ShapeDtypeStruct((NB * 24, 8, C), BF16)
    code = jax.ShapeDtypeStruct((1, 8, C), BF16)
    kept = tuple(jax.ShapeDtypeStruct(a.shape, a.dtype) for a in (x, g, w))
    return pl.pallas_call(
        stage_kernel,
        out_shape=kept + (code, beside, beside),
        in_specs=[SMEM, VMEM, VMEM, VMEM],
        out_specs=(VMEM,) * 6,
        compiler_params=small(4),
        name="stage",
    )(sites, x, g, w)


def pack_y_kernel(own_up, own_down, mine_ref, low_ref, high_ref, up_ref, down_ref):
    up_ref[: NB * 24] = own_up[...]
    down_ref[: NB * 24] = own_down[...]
    for side, ref in enumerate((low_ref, high_ref)):
        for s in range(NB):
            base = NB * 24 + 10 * side + 5 * s
            src = 24 * s
            for z in range(2):
                up_ref[base + 2 * z : base + 2 * z + 2] = ref[src + 8 * z + 6 : src + 8 * z + 8]
                down_ref[base + 2 * z : base + 2 * z + 2] = ref[src + 8 * z : src + 8 * z + 2]
            up_ref[base + 4] = ref[src + 16 + 7]
            down_ref[base + 4] = ref[src + 16]
    for k, row in enumerate((mine_ref[0], low_ref[Z_ROWS - 1], high_ref[Z_ROWS - 1])):
        up_ref[Y_ROWS - 3 + k] = row
        down_ref[Y_ROWS - 3 + k] = row


def pack_y(own_up, own_down, mine, low, high):
    shape = jax.ShapeDtypeStruct((Y_ROWS, 8, C), BF16)
    return pl.pallas_call(
        pack_y_kernel,
        out_shape=(shape, shape),
        in_specs=[VMEM] * 5,
        out_specs=(VMEM, VMEM),
        compiler_params=small(4),
        name="pack_y",
    )(own_up, own_down, mine, low, high)


def clear(ref):
    rows = ref.shape[0]
    flat = jnp.zeros((1,) + ref.shape[1:], ref.dtype)
    for z in range(rows):
        ref[z : z + 1] = flat


def place_of(site):
    inside = jnp.minimum(site, SITES - 1)
    return inside // BX, pl.multiple_of(inside % BX * 8 + 8, 8)


def read_codes(mine_ref, zl_ref, zh_ref, yl_ref, yh_ref):
    rows = [mine_ref[0], zl_ref[Z_ROWS - 1], zh_ref[Z_ROWS - 1]]
    rows += [ref[Y_ROWS - 3 + k] for ref in (yl_ref, yh_ref) for k in range(3)]
    codes = {}
    for k, row in enumerate(rows):
        row = row.astype(F32)
        for s in range(NB):
            codes[k, s] = SITES - row[0, s].astype(jnp.int32)
    return codes


def fill(vol, codes, x_ref, zl_ref, zh_ref, yl_ref, yh_ref):
    def put(z0, y0, x0, rows):
        vol[z0 : z0 + rows.shape[0], pl.ds(y0, rows.shape[1]), pl.ds(x0, 8)] = rows.astype(F32)

    for s in range(NB):
        site = codes[0, s]
        py, px = place_of(site)

        @pl.when(site < SITES)
        def _():
            put(2, 2 + 8 * py, px, x_ref[s])

        for side, ref in ((1, zl_ref), (2, zh_ref)):
            zsite = codes[side, s]
            zpy, zpx = place_of(zsite)

            @pl.when(zsite < SITES)
            def _(ref=ref, side=side, zpy=zpy, zpx=zpx, s=s):
                put(0 if side == 1 else 10, 2 + 8 * zpy, zpx, ref[24 * s : 24 * s + 16].reshape(2, 8, 8, C))

        for first, ref, row, y0 in ((3, yl_ref, 1, 0), (6, yh_ref, 0, 18)):
            for k, (z0, base, depth) in enumerate(
                ((2, 24 * s, 8), (0, 48 + 5 * s, 2), (10, 58 + 5 * s, 2))
            ):
                ysite = codes[first + k, s]
                ypy, ypx = place_of(ysite)

                @pl.when((ysite < SITES) & (ypy == row))
                def _(ref=ref, z0=z0, y0=y0, base=base, depth=depth, ypx=ypx):
                    put(z0, y0, ypx, ref[base : base + 2 * depth].reshape(depth, 2, 8, C))


def stack_x(vol, dst, dst_at, z0, y0s, x0s, nz, ny):
    for z in range(nz):
        for y in range(ny):
            halves = []
            for y0, x0 in zip(y0s, x0s):
                row = vol[z0 + z, y0 + y, pl.ds(x0 - 8, 24)]
                halves.append(
                    jnp.concatenate([row[7:15], row[8:16], row[9:17]], axis=1)
                )
            dst[dst_at + z * ny + y] = jnp.concatenate(halves, axis=0).astype(BF16)


def views(stack, base, ny_all, nz, ny):
    result = []
    for dz in range(3):
        for dy in range(3):
            planes = [
                stack[base + (z + dz) * ny_all + dy : base + (z + dz) * ny_all + dy + ny]
                for z in range(nz)
            ]
            result.append(jnp.concatenate(planes, axis=0).reshape(nz * ny * 16, 3 * C))
    return result


def dot(a, b, dims=((1,), (0,))):
    return lax.dot_general(a, b, (dims, ((), ())), preferred_element_type=F32)


def convolve(stack, base, ny_all, nz, ny, weight):
    total = None
    for k, view in enumerate(views(stack, base, ny_all, nz, ny)):
        term = weight(k, view)
        total = term if total is None else total + term
    return total


def forward_kernel(mine_ref, x_ref, g_ref, zl_ref, zh_ref, yl_ref, yh_ref, w_ref,
                   act_ref, dpre_ref, keep_ref, send_ref, vol, stack, turned, split):
    codes = read_codes(mine_ref, zl_ref, zh_ref, yl_ref, yh_ref)
    core = lax.axis_index("gy") & 1
    clear(vol)
    fill(vol, codes, x_ref, zl_ref, zh_ref, yl_ref, yh_ref)
    places = [place_of(codes[0, s]) for s in range(NB)]
    stack_x(vol, stack, 0, 1, [1 + 8 * py for py, _ in places], [px for _, px in places], 10, 10)

    def weight(k, view):
        return dot(view, w_ref[3 * k : 3 * k + 3].reshape(3 * C, C))

    used = [codes[0, s] < SITES for s in range(NB)]
    for half in range(2):
        pre = convolve(stack, 40 * half, 10, 4, 8, weight)
        sig = 1.0 / (1.0 + jnp.exp(-pre))
        act = (pre * sig).reshape(32, 16, C)
        slope = (sig * (1.0 + pre * (1.0 - sig))).reshape(32, 16, C)
        both = []
        for s in range(NB):
            rows = slice(32 * half, 32 * half + 32)
            a = jnp.where(used[s], act[:, 8 * s : 8 * s + 8], 0.0)
            act_ref[s, rows] = a.astype(BF16)
            d = g_ref[s, 4 * half : 4 * half + 4].astype(F32).reshape(32, 8, C) * slope[:, 8 * s : 8 * s + 8]
            both.append(jnp.where(used[s], d, 0.0))
        d = jnp.concatenate(both, axis=1).astype(BF16)
        dpre_ref[32 * half : 32 * half + 32] = d
        turned[:, 512 * half : 512 * half + 512] = d.reshape(512, C).T

    dt = turned[...]
    for k in range(9):
        dz, dy = divmod(k, 3)
        planes = [stack[(z + dz) * 10 + dy : (z + dz) * 10 + dy + 8] for z in range(8)]
        view = jnp.concatenate(planes, axis=0).reshape(1024, 3 * C)
        term = dot(dt, view)
        for dx in range(3):
            t = 3 * k + dx
            value = term[:, C * dx : C * dx + C].T
            half, at = divmod(t, HALF)
            split[(half ^ core) * HALF + at] = value
    for t in range(TAPS, 2 * HALF):
        half, at = divmod(t, HALF)
        split[(half ^ core) * HALF + at] = jnp.zeros((C, C), F32)
    keep_ref[...] = split[:HALF]
    send_ref[...] = split[HALF:].astype(BF16)


def forward(sites, x, g, zl, zh, yl, yh, w):
    rows = jax.ShapeDtypeStruct((NB, 64, 8, C), BF16)
    return pl.pallas_call(
        forward_kernel,
        out_shape=(
            rows,
            jax.ShapeDtypeStruct((64, 16, C), BF16),
            jax.ShapeDtypeStruct((HALF, C, C), F32),
            jax.ShapeDtypeStruct((HALF, C, C), BF16),
        ),
        in_specs=[VMEM] * 8,
        out_specs=(VMEM,) * 4,
        scratch_shapes=[
            pltpu.VMEM((VZ, VY, VX, C), F32),
            pltpu.VMEM((100, 16, 3 * C), BF16),
            pltpu.VMEM((C, 1024), BF16),
            pltpu.VMEM((2 * HALF, C, C), F32),
        ],
        compiler_params=small(18),
        cost_estimate=pl.CostEstimate(flops=2 * 10**9, bytes_accessed=5 << 20, transcendentals=1 << 17),
        name="forward",
    )(sites, x, g, zl, zh, yl, yh, w)


def backward_kernel(mine_ref, x_ref, dpre_ref, zl_ref, zh_ref, yl_ref, yh_ref, w_ref,
                    grad_ref, vol, stack):
    codes = read_codes(mine_ref, zl_ref, zh_ref, yl_ref, yh_ref)
    clear(vol)
    fill(vol, codes, x_ref, zl_ref, zh_ref, yl_ref, yh_ref)

    def weight(k, view):
        return dot(view, w_ref[3 * k : 3 * k + 3].reshape(3 * C, C))

    jobs = []
    for block, z in ((1, 1), (2, 10)):
        jobs.append((block, z, None, 1, 8))
    for first, y in ((3, 1), (6, 18)):
        jobs.append((first, 2, y, 8, 1))
        jobs.append((first + 1, 1, y, 1, 1))
        jobs.append((first + 2, 10, y, 1, 1))
    base = 0
    found = []
    for block, z0, y0, nz, ny in jobs:
        places = [place_of(codes[block, s]) for s in range(NB)]
        y0s = [2 + 8 * py if y0 is None else y0 for py, _ in places]
        x0s = [px for _, px in places]
        stack_x(vol, stack, base, z0 - 1, [y - 1 for y in y0s], x0s, nz + 2, ny + 2)
        pre = convolve(stack, base, ny + 2, nz, ny, weight)
        sig = 1.0 / (1.0 + jnp.exp(-pre))
        slope = (sig * (1.0 + pre * (1.0 - sig))).reshape(nz, ny, 16, C)
        found.append((block, z0, y0, nz, ny, y0s, x0s, slope))
        base += (nz + 2) * (ny + 2)
    values = []
    for block, z0, y0, nz, ny, y0s, x0s, slope in found:
        for s in range(NB):
            if block == 1:
                g = zl_ref[24 * s + 16 : 24 * s + 24]
            elif block == 2:
                g = zh_ref[24 * s + 16 : 24 * s + 24]
            else:
                ref = yl_ref if block < 6 else yh_ref
                kind = (block - 3) % 3
                if kind == 0:
                    g = ref[24 * s + 16 : 24 * s + 24]
                else:
                    at = 48 + 10 * (kind - 1) + 5 * s + 4
                    g = ref[at : at + 1]
            g = g.astype(F32).reshape(nz, ny, 8, C)
            value = (g * slope[:, :, 8 * s : 8 * s + 8]).astype(BF16).astype(F32)
            values.append(value)

    clear(vol)
    for s in range(NB):
        site = codes[0, s]
        py, px = place_of(site)

        @pl.when(site < SITES)
        def _(s=s, py=py, px=px):
            own = dpre_ref[...].astype(F32).reshape(8, 8, 16, C)[:, :, 8 * s : 8 * s + 8]
            vol[2:10, pl.ds(2 + 8 * py, 8), pl.ds(px, 8)] = own

    at = 0
    for block, z0, y0, nz, ny, y0s, x0s, slope in found:
        for s in range(NB):
            site = codes[block, s]
            py, px = place_of(site)
            ok = site < SITES
            if block >= 3:
                ok = ok & (py == (1 if block < 6 else 0))
            value = values[at]
            at += 1

            @pl.when(ok)
            def _(value=value, z0=z0, nz=nz, ny=ny, y0=y0s[s], x0=x0s[s]):
                vol[z0 : z0 + nz, pl.ds(y0, ny), pl.ds(x0, 8)] = value

    places = [place_of(codes[0, s]) for s in range(NB)]
    stack_x(vol, stack, 0, 1, [1 + 8 * py for py, _ in places], [px for _, px in places], 10, 10)

    def back(k, view):
        turned = [w_ref[26 - 3 * k - dx] for dx in range(3)]
        return dot(view, jnp.concatenate(turned, axis=1), ((1,), (1,)))

    for half in range(2):
        grad = convolve(stack, 40 * half, 10, 4, 8, back).reshape(32, 16, C)
        for s in range(NB):
            value = jnp.where(codes[0, s] < SITES, grad[:, 8 * s : 8 * s + 8], 0.0)
            grad_ref[s, 32 * half : 32 * half + 32] = value.astype(BF16)


def backward(sites, x, dpre, zl, zh, yl, yh, w):
    return pl.pallas_call(
        backward_kernel,
        out_shape=jax.ShapeDtypeStruct((NB, 64, 8, C), BF16),
        in_specs=[VMEM] * 8,
        out_specs=VMEM,
        scratch_shapes=[
            pltpu.VMEM((VZ, VY, VX, C), F32),
            pltpu.VMEM((160, 16, 3 * C), BF16),
        ],
        compiler_params=small(18),
        cost_estimate=pl.CostEstimate(flops=10**9, bytes_accessed=5 << 20, transcendentals=1 << 16),
        name="backward",
    )(sites, x, dpre, zl, zh, yl, yh, w)


def merge_kernel(group, scale, count, *refs):
    terms, outs = refs[:count], refs[count:]
    rows = outs[0].shape[0]
    me = place_in(group) if group else 0
    for p, out in enumerate(outs):
        at = pl.multiple_of((me ^ p) * rows, 16) if group else 0
        value = terms[0][pl.ds(at, rows)]
        for term in terms[1:]:
            value = value + term[pl.ds(at, rows)].astype(F32)
        out[...] = value if group and p == 0 else (value * scale).astype(BF16)


def merge(keep, arrived, group=None, scale=1.0):
    members = 1 << len(group) if group else 1
    shape = (keep.shape[0] // members, C)
    kinds = [F32] + [BF16] * (members - 1) if group else [BF16]
    return pl.pallas_call(
        functools.partial(merge_kernel, group, scale, 1 + len(arrived)),
        out_shape=tuple(jax.ShapeDtypeStruct(shape, kind) for kind in kinds),
        in_specs=[VMEM] * (1 + len(arrived)),
        out_specs=(VMEM,) * members,
        compiler_params=small(6),
        name="merge",
    )(keep, *arrived)


def join_kernel(*refs):
    out = refs[-1]
    for k, ref in enumerate(refs[:-1]):
        out[k * ref.shape[0] : (k + 1) * ref.shape[0]] = ref[...]


def join(pieces):
    rows = sum(p.shape[0] for p in pieces)
    return pl.pallas_call(
        join_kernel,
        out_shape=jax.ShapeDtypeStruct((rows, C), BF16),
        in_specs=[VMEM] * len(pieces),
        out_specs=VMEM,
        compiler_params=small(4),
        name="join",
    )(*pieces)


def finish_kernel(first, share, plan, *refs):
    pieces, out = refs[:-1], refs[-1]
    me = [place_in(group) for group in plan]
    sizes = [1 << len(group) for group in plan]
    middle, inner_sizes = sizes[1], sizes[2:]
    inner = 1
    for n in inner_sizes:
        inner *= n
    for k, ref in enumerate(pieces):
        half = (k // middle) ^ me[0]
        outer = (k % middle) ^ me[1]
        for r in range(inner):
            block, stride, rest = outer * inner, inner, r
            for level, n in enumerate(inner_sizes):
                stride //= n
                digit, rest = divmod(rest, stride)
                block = block + (digit ^ me[2 + level]) * stride
            value = ref[r * share : (r + 1) * share].astype(F32)
            for h in range(2):
                whole, rem = divmod(min(first, TAPS * C - h * first), share)

                @pl.when((half == h) & (block < whole))
                def _(value=value, h=h, block=block):
                    out[pl.ds(pl.multiple_of(h * first + block * share, 8), share)] = value

                if rem:

                    @pl.when((half == h) & (block == whole))
                    def _(value=value, h=h, whole=whole, rem=rem):
                        at = h * first + whole * share
                        out[at : at + rem] = value[:rem]


def finish(first, share, plan, pieces):
    return pl.pallas_call(
        functools.partial(finish_kernel, first, share, plan),
        out_shape=jax.ShapeDtypeStruct((TAPS * C, C), F32),
        in_specs=[VMEM] * len(pieces),
        out_specs=VMEM,
        compiler_params=small(8),
        name="finish",
    )(*pieces)


def local(features, brick_sites, kernel, cotangent):
    x = features.reshape(NB, 8, 8, 8, C)
    g = cotangent.reshape(NB, 8, 8, 8, C)
    sites = brick_sites.reshape(NB)
    devices = lax.axis_size("gz") * lax.axis_size("gy")
    z_up, z_down = pack_z(sites, x, g)
    z_up, z_down, *later = lax.optimization_barrier((z_up, z_down, sites, x, g, kernel))
    x, g, w, mine, own_up, own_down = stage(*later)
    zl, zh = neighbours(z_up, z_down, "gz")
    y_up, y_down = pack_y(own_up, own_down, mine, zl, zh)
    yl, yh = neighbours(y_up, y_down, "gy")
    act, dpre, keep, send = forward(mine, x, g, zl, zh, yl, yh, w)

    plan = exchange_plan()
    first = HALF * C
    sharers = devices // 2
    share = -(-first // (16 * sharers)) * 16
    half_rows = share * sharers
    arrived = swap_with(send, plan[0], 1)
    pad = ((0, half_rows - first), (0, 0))
    keep = jnp.pad(keep.reshape(first, C), pad)
    arrived = jnp.pad(arrived.reshape(first, C), pad)
    grad_in = None
    arrived = [arrived]
    for group in plan[1:]:
        keep, *sends = merge(keep, arrived, group)
        arrived = [swap_with(send, group, 1 + k) for k, send in enumerate(sends)]
        if grad_in is None:
            grad_in = backward(mine, x, dpre, zl, zh, yl, yh, w)
            *arrived, grad_in = lax.optimization_barrier((*arrived, grad_in))
    (piece,) = merge(keep, arrived, scale=1.0 / (NB * VOX * devices) ** 0.5)

    pieces = [piece]
    for level, group in enumerate(reversed(plan[1:])):
        if level > 0:
            pieces = [join(pieces)]
        pieces = [pieces[0]] + [swap_with(pieces[0], group, p) for p in range(1, 1 << len(group))]
    others = [swap_with(p, plan[0], 1) for p in pieces]
    grad_kernel = finish(first, share, plan, pieces + others)
    shape = (1, 1, NB, VOX, C)
    return act.reshape(shape), grad_in.reshape(shape), grad_kernel.reshape(TAPS, C, C)


def solution(mesh):
    placed = (
        P("gz", "gy", None, None, None),
        P("gz", "gy", None),
        P(),
        P("gz", "gy", None, None, None),
    )
    return jax.shard_map(
        local,
        mesh=mesh,
        in_specs=placed,
        out_specs=(P("gz", "gy", None, None, None), P("gz", "gy", None, None, None), P()),
        check_vma=False,
    )
```

```python
import functools

import jax
import jax.numpy as jnp
from jax import lax
from jax.experimental import pallas as pl
from jax.experimental.pallas import tpu as pltpu
from jax.sharding import PartitionSpec as P

C = 128
VOX = 512
BY = 2
BX = 4
NB = 2
SITES = 8
TAPS = 27
HALF = 14

AXES = ("gz", "gy")
F32 = jnp.float32
BF16 = jnp.bfloat16

VZ, VY, VX = 12, 20, 48

SMEM = pl.BlockSpec(memory_space=pltpu.SMEM)
VMEM = pl.BlockSpec(memory_space=pltpu.VMEM)
ANY = pl.BlockSpec(memory_space=pl.ANY)


def exchange_plan():
    gz_bits = [("gz", b) for b in range(lax.axis_size("gz").bit_length() - 1)]
    gy_bits = [("gy", b) for b in range(lax.axis_size("gy").bit_length() - 1)]
    groups, gy_bits = [(gy_bits[0],)], gy_bits[1:]
    while gy_bits and gz_bits:
        groups.append((gy_bits.pop(0), gz_bits.pop(0)))
    rest = gy_bits + gz_bits
    while rest:
        groups.append(tuple(rest[:2]))
        rest = rest[2:]
    return groups


def swap_with(value, group, pattern):
    nz, ny = lax.axis_size("gz"), lax.axis_size("gy")
    flip = {"gz": 0, "gy": 0}
    for k, (axis, bit) in enumerate(group):
        if pattern >> k & 1:
            flip[axis] |= 1 << bit
    pairs = [
        (z * ny + y, (z ^ flip["gz"]) * ny + (y ^ flip["gy"]))
        for z in range(nz)
        for y in range(ny)
    ]
    return lax.ppermute(value, AXES, pairs)


def place_in(group):
    place = jnp.zeros((), jnp.int32)
    for k, (axis, bit) in enumerate(group):
        place = place | (((lax.axis_index(axis) >> bit) & 1) << k)
    return place


def neighbours(up, down, axis):
    count = lax.axis_size(axis)
    forward = [(i, i + 1) for i in range(count - 1)]
    backward = [(b, a) for a, b in forward]
    return lax.ppermute(up, axis, forward), lax.ppermute(down, axis, backward)


Z_ROWS = NB * 24 + 1
Y_ROWS = NB * 24 + 2 * NB * 5 + 3


def code_row(sites):
    lane = lax.broadcasted_iota(jnp.int32, (8, C), 1)
    code = jnp.zeros((8, C), jnp.int32)
    for s in range(NB):
        code = jnp.where(lane == s, SITES - sites[s], code)
    return code.astype(F32).astype(BF16)


def pack_z_kernel(sites_ref, x_ref, g_ref, up_ref, down_ref, sites, sems):
    moves = [(sites_ref, sites)]
    for s in range(NB):
        base = 24 * s
        first, last = slice(base, base + 16), slice(base + 16, base + 24)
        moves += [
            (x_ref.at[s, 6:8], up_ref.at[first].reshape(2, 8, 8, C)),
            (g_ref.at[s, 7], up_ref.at[last]),
            (x_ref.at[s, 0:2], down_ref.at[first].reshape(2, 8, 8, C)),
            (g_ref.at[s, 0], down_ref.at[last]),
        ]
    copies = [
        pltpu.make_async_copy(src, dst, sems.at[k]) for k, (src, dst) in enumerate(moves)
    ]
    for copy in copies:
        copy.start()
    copies[0].wait()
    code = code_row(sites)
    up_ref[Z_ROWS - 1] = code
    down_ref[Z_ROWS - 1] = code
    for copy in copies[1:]:
        copy.wait()


def small(limit):
    return pltpu.CompilerParams(vmem_limit_bytes=limit << 20)


def pack_z(sites, x, g):
    shape = jax.ShapeDtypeStruct((Z_ROWS, 8, C), BF16)
    return pl.pallas_call(
        pack_z_kernel,
        out_shape=(shape, shape),
        in_specs=[ANY, ANY, ANY],
        out_specs=(VMEM,) * 2,
        scratch_shapes=[pltpu.SMEM((NB,), jnp.int32), pltpu.SemaphoreType.DMA((1 + 4 * NB,))],
        compiler_params=pltpu.CompilerParams(vmem_limit_bytes=67043328),
        name="pack_z",
    )(sites, x, g)


def stage_kernel(sites, x_ref, g_ref, x_out, g_out, code_out, up_ref, down_ref):
    x_out[...] = x_ref[...]
    g_out[...] = g_ref[...]
    code_out[0] = code_row(sites)
    for s in range(NB):
        first, last = slice(24 * s, 24 * s + 16), slice(24 * s + 16, 24 * s + 24)
        up_ref[first] = x_ref[s, :, 6:8].reshape(16, 8, C)
        up_ref[last] = g_ref[s, :, 7]
        down_ref[first] = x_ref[s, :, 0:2].reshape(16, 8, C)
        down_ref[last] = g_ref[s, :, 0]


def stage(sites, x, g):
    beside = jax.ShapeDtypeStruct((NB * 24, 8, C), BF16)
    code = jax.ShapeDtypeStruct((1, 8, C), BF16)
    kept = tuple(jax.ShapeDtypeStruct(a.shape, a.dtype) for a in (x, g))
    return pl.pallas_call(
        stage_kernel,
        out_shape=kept + (code, beside, beside),
        in_specs=[SMEM, VMEM, VMEM],
        out_specs=(VMEM,) * 5,
        compiler_params=small(4),
        name="stage",
    )(sites, x, g)


def keep_kernel(w_ref, w_out):
    w_out[...] = w_ref[...]


def keep_near(w):
    return pl.pallas_call(
        keep_kernel,
        out_shape=jax.ShapeDtypeStruct(w.shape, w.dtype),
        in_specs=[VMEM],
        out_specs=VMEM,
        compiler_params=small(4),
        name="keep_near",
    )(w)


def pack_y_kernel(own_up, own_down, mine_ref, low_ref, high_ref, up_ref, down_ref):
    up_ref[: NB * 24] = own_up[...]
    down_ref[: NB * 24] = own_down[...]
    for side, ref in enumerate((low_ref, high_ref)):
        for s in range(NB):
            base = NB * 24 + 10 * side + 5 * s
            src = 24 * s
            for z in range(2):
                up_ref[base + 2 * z : base + 2 * z + 2] = ref[src + 8 * z + 6 : src + 8 * z + 8]
                down_ref[base + 2 * z : base + 2 * z + 2] = ref[src + 8 * z : src + 8 * z + 2]
            up_ref[base + 4] = ref[src + 16 + 7]
            down_ref[base + 4] = ref[src + 16]
    for k, row in enumerate((mine_ref[0], low_ref[Z_ROWS - 1], high_ref[Z_ROWS - 1])):
        up_ref[Y_ROWS - 3 + k] = row
        down_ref[Y_ROWS - 3 + k] = row


def pack_y(own_up, own_down, mine, low, high):
    shape = jax.ShapeDtypeStruct((Y_ROWS, 8, C), BF16)
    return pl.pallas_call(
        pack_y_kernel,
        out_shape=(shape, shape),
        in_specs=[VMEM] * 5,
        out_specs=(VMEM, VMEM),
        compiler_params=small(4),
        name="pack_y",
    )(own_up, own_down, mine, low, high)


def clear(ref):
    rows = ref.shape[0]
    flat = jnp.zeros((1,) + ref.shape[1:], ref.dtype)
    for z in range(rows):
        ref[z : z + 1] = flat


def place_of(site):
    inside = jnp.minimum(site, SITES - 1)
    return inside // BX, pl.multiple_of(inside % BX * 8 + 8, 8)


def read_codes(mine_ref, zl_ref, zh_ref, yl_ref, yh_ref):
    rows = [mine_ref[0], zl_ref[Z_ROWS - 1], zh_ref[Z_ROWS - 1]]
    rows += [ref[Y_ROWS - 3 + k] for ref in (yl_ref, yh_ref) for k in range(3)]
    codes = {}
    for k, row in enumerate(rows):
        row = row.astype(F32)
        for s in range(NB):
            codes[k, s] = SITES - row[0, s].astype(jnp.int32)
    return codes


def fill(vol, codes, x_ref, zl_ref, zh_ref, yl_ref, yh_ref):
    def put(z0, y0, x0, rows):
        vol[z0 : z0 + rows.shape[0], pl.ds(y0, rows.shape[1]), pl.ds(x0, 8)] = rows.astype(F32)

    for s in range(NB):
        site = codes[0, s]
        py, px = place_of(site)

        @pl.when(site < SITES)
        def _():
            put(2, 2 + 8 * py, px, x_ref[s])

        for side, ref in ((1, zl_ref), (2, zh_ref)):
            zsite = codes[side, s]
            zpy, zpx = place_of(zsite)

            @pl.when(zsite < SITES)
            def _(ref=ref, side=side, zpy=zpy, zpx=zpx, s=s):
                put(0 if side == 1 else 10, 2 + 8 * zpy, zpx, ref[24 * s : 24 * s + 16].reshape(2, 8, 8, C))

        for first, ref, row, y0 in ((3, yl_ref, 1, 0), (6, yh_ref, 0, 18)):
            for k, (z0, base, depth) in enumerate(
                ((2, 24 * s, 8), (0, 48 + 5 * s, 2), (10, 58 + 5 * s, 2))
            ):
                ysite = codes[first + k, s]
                ypy, ypx = place_of(ysite)

                @pl.when((ysite < SITES) & (ypy == row))
                def _(ref=ref, z0=z0, y0=y0, base=base, depth=depth, ypx=ypx):
                    put(z0, y0, ypx, ref[base : base + 2 * depth].reshape(depth, 2, 8, C))


def stack_x(vol, dst, dst_at, z0, y0s, x0s, nz, ny):
    for z in range(nz):
        for y in range(ny):
            halves = []
            for y0, x0 in zip(y0s, x0s):
                row = vol[z0 + z, y0 + y, pl.ds(x0 - 8, 24)]
                halves.append(
                    jnp.concatenate([row[7:15], row[8:16], row[9:17]], axis=1)
                )
            dst[dst_at + z * ny + y] = jnp.concatenate(halves, axis=0).astype(BF16)


def views(stack, base, ny_all, nz, ny):
    result = []
    for dz in range(3):
        for dy in range(3):
            planes = [
                stack[base + (z + dz) * ny_all + dy : base + (z + dz) * ny_all + dy + ny]
                for z in range(nz)
            ]
            result.append(jnp.concatenate(planes, axis=0).reshape(nz * ny * 16, 3 * C))
    return result


def dot(a, b, dims=((1,), (0,))):
    return lax.dot_general(a, b, (dims, ((), ())), preferred_element_type=F32)


def convolve(stack, base, ny_all, nz, ny, weight):
    total = None
    for k, view in enumerate(views(stack, base, ny_all, nz, ny)):
        term = weight(k, view)
        total = term if total is None else total + term
    return total


def forward_kernel(mine_ref, x_ref, g_ref, zl_ref, zh_ref, yl_ref, yh_ref, w_ref,
                   act_ref, dpre_ref, keep_ref, send_ref, vol, stack, turned, split):
    codes = read_codes(mine_ref, zl_ref, zh_ref, yl_ref, yh_ref)
    core = lax.axis_index("gy") & 1
    clear(vol)
    fill(vol, codes, x_ref, zl_ref, zh_ref, yl_ref, yh_ref)
    places = [place_of(codes[0, s]) for s in range(NB)]
    stack_x(vol, stack, 0, 1, [1 + 8 * py for py, _ in places], [px for _, px in places], 10, 10)

    def weight(k, view):
        return dot(view, w_ref[3 * k : 3 * k + 3].reshape(3 * C, C))

    used = [codes[0, s] < SITES for s in range(NB)]
    for half in range(2):
        pre = convolve(stack, 40 * half, 10, 4, 8, weight)
        sig = 1.0 / (1.0 + jnp.exp(-pre))
        act = (pre * sig).reshape(32, 16, C)
        slope = (sig * (1.0 + pre * (1.0 - sig))).reshape(32, 16, C)
        both = []
        for s in range(NB):
            rows = slice(32 * half, 32 * half + 32)
            a = jnp.where(used[s], act[:, 8 * s : 8 * s + 8], 0.0)
            act_ref[s, rows] = a.astype(BF16)
            d = g_ref[s, 4 * half : 4 * half + 4].astype(F32).reshape(32, 8, C) * slope[:, 8 * s : 8 * s + 8]
            both.append(jnp.where(used[s], d, 0.0))
        d = jnp.concatenate(both, axis=1).astype(BF16)
        dpre_ref[32 * half : 32 * half + 32] = d
        turned[:, 512 * half : 512 * half + 512] = d.reshape(512, C).T

    dt = turned[...]
    for k in range(9):
        dz, dy = divmod(k, 3)
        planes = [stack[(z + dz) * 10 + dy : (z + dz) * 10 + dy + 8] for z in range(8)]
        view = jnp.concatenate(planes, axis=0).reshape(1024, 3 * C)
        term = dot(dt, view)
        for dx in range(3):
            t = 3 * k + dx
            value = term[:, C * dx : C * dx + C].T
            half, at = divmod(t, HALF)
            split[(half ^ core) * HALF + at] = value
    for t in range(TAPS, 2 * HALF):
        half, at = divmod(t, HALF)
        split[(half ^ core) * HALF + at] = jnp.zeros((C, C), F32)
    keep_ref[...] = split[:HALF]
    send_ref[...] = split[HALF:].astype(BF16)


def forward(sites, x, g, zl, zh, yl, yh, w):
    rows = jax.ShapeDtypeStruct((NB, 64, 8, C), BF16)
    return pl.pallas_call(
        forward_kernel,
        out_shape=(
            rows,
            jax.ShapeDtypeStruct((64, 16, C), BF16),
            jax.ShapeDtypeStruct((HALF, C, C), F32),
            jax.ShapeDtypeStruct((HALF, C, C), BF16),
        ),
        in_specs=[VMEM] * 8,
        out_specs=(VMEM,) * 4,
        scratch_shapes=[
            pltpu.VMEM((VZ, VY, VX, C), F32),
            pltpu.VMEM((100, 16, 3 * C), BF16),
            pltpu.VMEM((C, 1024), BF16),
            pltpu.VMEM((2 * HALF, C, C), F32),
        ],
        compiler_params=small(18),
        cost_estimate=pl.CostEstimate(flops=2 * 10**9, bytes_accessed=5 << 20, transcendentals=1 << 17),
        name="forward",
    )(sites, x, g, zl, zh, yl, yh, w)


def backward_kernel(mine_ref, x_ref, dpre_ref, zl_ref, zh_ref, yl_ref, yh_ref, w_ref,
                    grad_ref, vol, stack):
    codes = read_codes(mine_ref, zl_ref, zh_ref, yl_ref, yh_ref)
    clear(vol)
    fill(vol, codes, x_ref, zl_ref, zh_ref, yl_ref, yh_ref)

    def weight(k, view):
        return dot(view, w_ref[3 * k : 3 * k + 3].reshape(3 * C, C))

    jobs = []
    for block, z in ((1, 1), (2, 10)):
        jobs.append((block, z, None, 1, 8))
    for first, y in ((3, 1), (6, 18)):
        jobs.append((first, 2, y, 8, 1))
        jobs.append((first + 1, 1, y, 1, 1))
        jobs.append((first + 2, 10, y, 1, 1))
    base = 0
    found = []
    for block, z0, y0, nz, ny in jobs:
        places = [place_of(codes[block, s]) for s in range(NB)]
        y0s = [2 + 8 * py if y0 is None else y0 for py, _ in places]
        x0s = [px for _, px in places]
        stack_x(vol, stack, base, z0 - 1, [y - 1 for y in y0s], x0s, nz + 2, ny + 2)
        pre = convolve(stack, base, ny + 2, nz, ny, weight)
        sig = 1.0 / (1.0 + jnp.exp(-pre))
        slope = (sig * (1.0 + pre * (1.0 - sig))).reshape(nz, ny, 16, C)
        found.append((block, z0, y0, nz, ny, y0s, x0s, slope))
        base += (nz + 2) * (ny + 2)
    values = []
    for block, z0, y0, nz, ny, y0s, x0s, slope in found:
        for s in range(NB):
            if block == 1:
                g = zl_ref[24 * s + 16 : 24 * s + 24]
            elif block == 2:
                g = zh_ref[24 * s + 16 : 24 * s + 24]
            else:
                ref = yl_ref if block < 6 else yh_ref
                kind = (block - 3) % 3
                if kind == 0:
                    g = ref[24 * s + 16 : 24 * s + 24]
                else:
                    at = 48 + 10 * (kind - 1) + 5 * s + 4
                    g = ref[at : at + 1]
            g = g.astype(F32).reshape(nz, ny, 8, C)
            value = (g * slope[:, :, 8 * s : 8 * s + 8]).astype(BF16).astype(F32)
            values.append(value)

    clear(vol)
    for s in range(NB):
        site = codes[0, s]
        py, px = place_of(site)

        @pl.when(site < SITES)
        def _(s=s, py=py, px=px):
            own = dpre_ref[...].astype(F32).reshape(8, 8, 16, C)[:, :, 8 * s : 8 * s + 8]
            vol[2:10, pl.ds(2 + 8 * py, 8), pl.ds(px, 8)] = own

    at = 0
    for block, z0, y0, nz, ny, y0s, x0s, slope in found:
        for s in range(NB):
            site = codes[block, s]
            py, px = place_of(site)
            ok = site < SITES
            if block >= 3:
                ok = ok & (py == (1 if block < 6 else 0))
            value = values[at]
            at += 1

            @pl.when(ok)
            def _(value=value, z0=z0, nz=nz, ny=ny, y0=y0s[s], x0=x0s[s]):
                vol[z0 : z0 + nz, pl.ds(y0, ny), pl.ds(x0, 8)] = value

    places = [place_of(codes[0, s]) for s in range(NB)]
    stack_x(vol, stack, 0, 1, [1 + 8 * py for py, _ in places], [px for _, px in places], 10, 10)

    def back(k, view):
        turned = [w_ref[26 - 3 * k - dx] for dx in range(3)]
        return dot(view, jnp.concatenate(turned, axis=1), ((1,), (1,)))

    for half in range(2):
        grad = convolve(stack, 40 * half, 10, 4, 8, back).reshape(32, 16, C)
        for s in range(NB):
            value = jnp.where(codes[0, s] < SITES, grad[:, 8 * s : 8 * s + 8], 0.0)
            grad_ref[s, 32 * half : 32 * half + 32] = value.astype(BF16)


def backward(sites, x, dpre, zl, zh, yl, yh, w):
    return pl.pallas_call(
        backward_kernel,
        out_shape=jax.ShapeDtypeStruct((NB, 64, 8, C), BF16),
        in_specs=[VMEM] * 8,
        out_specs=VMEM,
        scratch_shapes=[
            pltpu.VMEM((VZ, VY, VX, C), F32),
            pltpu.VMEM((160, 16, 3 * C), BF16),
        ],
        compiler_params=small(18),
        cost_estimate=pl.CostEstimate(flops=10**9, bytes_accessed=5 << 20, transcendentals=1 << 16),
        name="backward",
    )(sites, x, dpre, zl, zh, yl, yh, w)


def merge_kernel(group, scale, count, *refs):
    terms, outs = refs[:count], refs[count:]
    rows = outs[0].shape[0]
    me = place_in(group) if group else 0
    for p, out in enumerate(outs):
        at = pl.multiple_of((me ^ p) * rows, 16) if group else 0
        value = terms[0][pl.ds(at, rows)]
        for term in terms[1:]:
            value = value + term[pl.ds(at, rows)].astype(F32)
        out[...] = value if group and p == 0 else (value * scale).astype(BF16)


def merge(keep, arrived, group=None, scale=1.0):
    members = 1 << len(group) if group else 1
    shape = (keep.shape[0] // members, C)
    kinds = [F32] + [BF16] * (members - 1) if group else [BF16]
    return pl.pallas_call(
        functools.partial(merge_kernel, group, scale, 1 + len(arrived)),
        out_shape=tuple(jax.ShapeDtypeStruct(shape, kind) for kind in kinds),
        in_specs=[VMEM] * (1 + len(arrived)),
        out_specs=(VMEM,) * members,
        compiler_params=small(6),
        name="merge",
    )(keep, *arrived)


def join_kernel(*refs):
    out = refs[-1]
    for k, ref in enumerate(refs[:-1]):
        out[k * ref.shape[0] : (k + 1) * ref.shape[0]] = ref[...]


def join(pieces):
    rows = sum(p.shape[0] for p in pieces)
    return pl.pallas_call(
        join_kernel,
        out_shape=jax.ShapeDtypeStruct((rows, C), BF16),
        in_specs=[VMEM] * len(pieces),
        out_specs=VMEM,
        compiler_params=small(4),
        name="join",
    )(*pieces)


def finish_kernel(first, share, plan, *refs):
    pieces, out = refs[:-1], refs[-1]
    me = [place_in(group) for group in plan]
    sizes = [1 << len(group) for group in plan]
    middle, inner_sizes = sizes[1], sizes[2:]
    inner = 1
    for n in inner_sizes:
        inner *= n
    for k, ref in enumerate(pieces):
        half = (k // middle) ^ me[0]
        outer = (k % middle) ^ me[1]
        for r in range(inner):
            block, stride, rest = outer * inner, inner, r
            for level, n in enumerate(inner_sizes):
                stride //= n
                digit, rest = divmod(rest, stride)
                block = block + (digit ^ me[2 + level]) * stride
            value = ref[r * share : (r + 1) * share].astype(F32)
            for h in range(2):
                whole, rem = divmod(min(first, TAPS * C - h * first), share)

                @pl.when((half == h) & (block < whole))
                def _(value=value, h=h, block=block):
                    out[pl.ds(pl.multiple_of(h * first + block * share, 8), share)] = value

                if rem:

                    @pl.when((half == h) & (block == whole))
                    def _(value=value, h=h, whole=whole, rem=rem):
                        at = h * first + whole * share
                        out[at : at + rem] = value[:rem]


def finish(first, share, plan, pieces):
    return pl.pallas_call(
        functools.partial(finish_kernel, first, share, plan),
        out_shape=jax.ShapeDtypeStruct((TAPS * C, C), F32),
        in_specs=[VMEM] * len(pieces),
        out_specs=VMEM,
        compiler_params=small(8),
        name="finish",
    )(*pieces)


def local(features, brick_sites, kernel, cotangent):
    x = features.reshape(NB, 8, 8, 8, C)
    g = cotangent.reshape(NB, 8, 8, 8, C)
    sites = brick_sites.reshape(NB)
    devices = lax.axis_size("gz") * lax.axis_size("gy")
    z_up, z_down = pack_z(sites, x, g)
    z_up, z_down, *later = lax.optimization_barrier((z_up, z_down, sites, x, g))
    x, g, mine, own_up, own_down = stage(*later)
    zl, zh = neighbours(z_up, z_down, "gz")
    y_up, y_down = pack_y(own_up, own_down, mine, zl, zh)
    y_up, y_down, w = lax.optimization_barrier((y_up, y_down, kernel))
    w = keep_near(w)
    yl, yh = neighbours(y_up, y_down, "gy")
    act, dpre, keep, send = forward(mine, x, g, zl, zh, yl, yh, w)

    plan = exchange_plan()
    first = HALF * C
    sharers = devices // 2
    share = -(-first // (16 * sharers)) * 16
    half_rows = share * sharers
    arrived = swap_with(send, plan[0], 1)
    pad = ((0, half_rows - first), (0, 0))
    keep = jnp.pad(keep.reshape(first, C), pad)
    arrived = jnp.pad(arrived.reshape(first, C), pad)
    grad_in = None
    arrived = [arrived]
    for group in plan[1:]:
        keep, *sends = merge(keep, arrived, group)
        arrived = [swap_with(send, group, 1 + k) for k, send in enumerate(sends)]
        if grad_in is None:
            grad_in = backward(mine, x, dpre, zl, zh, yl, yh, w)
            *arrived, grad_in = lax.optimization_barrier((*arrived, grad_in))
    (piece,) = merge(keep, arrived, scale=1.0 / (NB * VOX * devices) ** 0.5)

    pieces = [piece]
    for level, group in enumerate(reversed(plan[1:])):
        if level > 0:
            pieces = [join(pieces)]
        pieces = [pieces[0]] + [swap_with(pieces[0], group, p) for p in range(1, 1 << len(group))]
    others = [swap_with(p, plan[0], 1) for p in pieces]
    grad_kernel = finish(first, share, plan, pieces + others)
    shape = (1, 1, NB, VOX, C)
    return act.reshape(shape), grad_in.reshape(shape), grad_kernel.reshape(TAPS, C, C)


def solution(mesh):
    placed = (
        P("gz", "gy", None, None, None),
        P("gz", "gy", None),
        P(),
        P("gz", "gy", None, None, None),
    )
    return jax.shard_map(
        local,
        mesh=mesh,
        in_specs=placed,
        out_specs=(P("gz", "gy", None, None, None), P("gz", "gy", None, None, None), P()),
        check_vma=False,
    )
```
